512 devices in a mesh: wide: 64 (over y_hi, x, z), narrow: 8 (over y_lo, core).
Axes of the slice: x: 4, y: 8 (y_hi: 2, y_lo: 4; y = y_hi * 4 + y_lo), z: 8, core: 2. Of those that a mesh axis runs over, the one named last changes fastest.
Arguments:
- features: bfloat16 [65536, 1792], P(('wide', 'narrow')), may hold values from -6 to 6
- weight: bfloat16 [1792, 512], replicated, may hold values from -0.125 to 0.125
- bias: float32 [512], replicated, may hold values from -3 to 3
- tile_cols: int32 [512, 24], P(('wide', 'narrow')), may hold values from 0 to 511, as said below
- tile_count: int32 [512], P(('wide', 'narrow')), may hold values from 8 to 24, as said below
- nbr_slot: int32 [65536, 15], P(('wide', 'narrow')), may hold values from 0 to 23
- nbr_col: int32 [65536, 15], P(('wide', 'narrow')), may hold values from 0 to 127
- nbr_keep: int32 [65536, 15], P(('wide', 'narrow')), may hold values 0 or 1
- upstream: bfloat16 [65536, 512], P(('wide', 'narrow')), may hold values from -6 to 6
Outputs:
- hidden: bfloat16 [65536, 512], P(('wide', 'narrow'))
- grad_features: bfloat16 [65536, 1792], P(('wide', 'narrow'))
- grad_weight: bfloat16 [1792, 512], replicated
- grad_bias: float32 [512], replicated
The draws below stay inside these ranges and needn't reach their ends.
Inputs may be any that keep to these rules, and one draw needn't show every extreme that they name: `tile_cols`: each block row lists 24 different column blocks, all in the wide group of the block row itself or in the two wide groups beside it, the first and last groups being beside each other. `tile_count`: some block row stores all 24 slots.
All inputs are finite; a program needn't handle non-finite values. No bound on the sum of `nbr_keep` on one device may be relied on, other than what follows from the above.
Results may differ from the reference program's by a relative error of at most 0.01.
Values may be sent and summed in bfloat16 or wider, within the bound.
No kernel may reach another device: no remote copies, remote signals or barrier semaphores. Data moves between devices by JAX's collectives and lax.ppermute only.
A program may use at most 64 MiB of HBM per device.

```python
import jax
import jax.numpy as jnp

F_IN = 1792
HID = 512
TILE = 128
KNN = 15
KMAX = 24
NBLK = 512
NODES = 65536


def draw_tile_cols(key, part):
    group_blocks = KMAX // 3
    row_keys = jax.random.split(key, NBLK)
    order = jax.vmap(lambda row_key: jax.random.permutation(row_key, KMAX))(row_keys).astype(jnp.int32)
    block_ids = jnp.arange(NBLK, dtype=jnp.int32)
    start = (block_ids // group_blocks - 1) * group_blocks
    return ((start[:, None] + order) % NBLK).astype(jnp.int32)


def draw_tile_count(key, part):
    lowest = max(1, KMAX // 3)
    counts = jax.random.randint(key, (NBLK,), lowest, KMAX + 1).astype(jnp.int32)
    chosen_row = jax.random.randint(jax.random.fold_in(key, 7), (), 0, NBLK)
    return counts.at[chosen_row].set(KMAX).astype(jnp.int32)


def set_ends(values, stream_key, least, high):
    spot = [jax.random.randint(jax.random.fold_in(stream_key, axis), (), 0, length) for axis, length in enumerate(values.shape)]
    main_axis = values.shape.index(max(values.shape))
    next_to = spot[:main_axis] + [(spot[main_axis] + 1) % values.shape[main_axis]] + spot[main_axis + 1:]
    return values.at[tuple(spot)].set(least).at[tuple(next_to)].set(high)


def level_of(own_key, shape, cuts, least, top_value):
    def one(dim, parts):
        draws = jax.random.uniform(jax.random.fold_in(jax.random.fold_in(own_key, 6), dim), (parts,), jnp.float32, least / len(cuts), top_value / len(cuts))
        return jnp.repeat(jnp.exp(draws), shape[dim] // parts).reshape((-1,) + (1,) * (len(shape) - dim - 1))

    factor_of = one(*cuts[0])
    for cut in cuts[1:]:
        factor_of = factor_of * one(*cut)
    return factor_of


def scatter_about(own_key, dims, deviation, reach, shards=(), kind=jnp.bfloat16):
    values = deviation * jax.random.normal(own_key, dims, jnp.float32)
    if shards:
        values = values * level_of(own_key, dims, shards, -0.22, 0.18)
    return jnp.clip(values, -reach, reach).astype(kind)


def setup_inputs(seed: int = 0) -> dict:
    arg_keys = jax.random.split(jax.random.key(seed), 10)
    return {
        "features": scatter_about(arg_keys[0], (NODES, F_IN), 1.0, 6.0, ((0, 512),)),
        "weight": scatter_about(arg_keys[1], (F_IN, HID), F_IN ** -0.5, 0.125),
        "bias": scatter_about(arg_keys[2], (HID,), 0.5, 3.0, (), jnp.float32),
        "tile_cols": draw_tile_cols(jax.random.fold_in(arg_keys[9], 71), 0),
        "tile_count": draw_tile_count(jax.random.fold_in(arg_keys[9], 71), 0),
        "nbr_slot": set_ends(jax.random.randint(arg_keys[5], (NODES, KNN), 0, KMAX), jax.random.fold_in(arg_keys[5], 1), 0, KMAX - 1).astype(jnp.int32),
        "nbr_col": set_ends(jax.random.randint(arg_keys[6], (NODES, KNN), 0, TILE), jax.random.fold_in(arg_keys[6], 1), 0, TILE - 1).astype(jnp.int32),
        "nbr_keep": set_ends((jax.random.randint(arg_keys[7], (NODES, KNN), 0, 5) < 4).astype(jnp.int32), jax.random.fold_in(arg_keys[7], 1), 0, 1),
        "upstream": scatter_about(arg_keys[8], (NODES, HID), 1.0, 6.0, ((0, 512),)),
    }


def reference(features, weight, bias, tile_cols, tile_count, nbr_slot, nbr_col, nbr_keep, upstream):
    projected = jnp.dot(features, weight, preferred_element_type=jnp.float32).astype(jnp.bfloat16)
    block_of = (jnp.arange(NODES, dtype=jnp.int32) // TILE).astype(jnp.int32)
    row_tiles = tile_cols[block_of]
    chosen = jnp.take_along_axis(row_tiles, nbr_slot, axis=1)
    col_id = (chosen * TILE + nbr_col).astype(jnp.int32)
    row_count = tile_count[block_of]
    live = nbr_keep * (nbr_slot < row_count[:, None]).astype(jnp.int32)
    live_float = live.astype(jnp.float32)
    degree = 1.0 + jnp.sum(live_float, axis=1)
    proj_float = projected.astype(jnp.float32)
    total = proj_float
    for edge in range(KNN):
        total = total + live_float[:, edge:edge + 1] * proj_float[col_id[:, edge]]
    pre_activation = total / degree[:, None] + bias
    sigma_pre = jax.nn.sigmoid(pre_activation)
    hidden = (pre_activation * sigma_pre).astype(jnp.bfloat16)
    grad_pre = upstream.astype(jnp.float32) * sigma_pre * (1.0 + pre_activation * (1.0 - sigma_pre))
    scaled = (grad_pre / degree[:, None]).astype(jnp.bfloat16)
    scaled_float = scaled.astype(jnp.float32)
    grad_proj = scaled_float
    for edge in range(KNN):
        grad_proj = grad_proj.at[col_id[:, edge]].add(live_float[:, edge:edge + 1] * scaled_float)
    grad_round = grad_proj.astype(jnp.bfloat16)
    grad_weight = jnp.dot(features.T, grad_round, preferred_element_type=jnp.float32).astype(jnp.bfloat16)
    grad_bias = jnp.sum(grad_pre, axis=0)
    grad_features = jnp.dot(grad_round, weight.T, preferred_element_type=jnp.float32).astype(jnp.bfloat16)
    return hidden, grad_features, grad_weight, grad_bias
```

```python
import jax
import jax.numpy as jnp
from jax import lax
from jax.experimental import pallas as pl
from jax.experimental.pallas import tpu as pltpu
from jax.sharding import Mesh
from jax.sharding import PartitionSpec as P

TILE = 128
KNN = 15
HID = 512
AXES = ("yh", "x", "z", "yl", "c")
SIZES = (2, 4, 8, 4, 2)
WIDE = ("yh", "x", "z")
RUN = 4
PARITY_ROWS = RUN * TILE
KEY_ROWS = 8
DEAD = 31
PIECES = 6
F_RUN = 448
SLABS = 128
BIAS_SLAB = 112

bf16 = jnp.bfloat16
f32 = jnp.float32


def spread_to(shard, axes, count):
    return lax.all_to_all(jnp.broadcast_to(shard[None], (count,) + shard.shape), axes, 0, 0)


def neighbours(block):
    count = 64
    forward = [(i, (i + 1) % count) for i in range(count)]
    backward = [((i + 1) % count, i) for i in range(count)]
    return lax.ppermute(block, WIDE, forward), lax.ppermute(block, WIDE, backward)


def swap_core(block):
    return lax.ppermute(block, "c", [(0, 1), (1, 0)])


def gather_window(shard):
    own = spread_to(shard, "yl", RUN)
    low, high = neighbours(own)
    own_other = swap_core(own)
    return low, swap_core(low), own, own_other, high, swap_core(high)


def forward_counts_kernel(key_ref, out_ref):
    def rows(step, carry):
        keys = key_ref[pl.ds(step * 16, 16), :]
        spread = [jnp.broadcast_to(keys[:, e : e + 1], (16, 128)) for e in range(KNN)]
        for tile in range(PIECES * RUN):
            lanes = lax.broadcasted_iota(jnp.int32, (16, 128), 1) + tile * 128
            total = jnp.zeros((16, 128), f32)
            for e in range(KNN):
                total = total + jnp.where(spread[e] == lanes, 1.0, 0.0)
            out_ref[pl.ds(step * 16, 16), tile * 128 : (tile + 1) * 128] = total.astype(bf16)
        return carry

    lax.fori_loop(0, TILE // 16, rows, 0)


def forward_counts(keys):
    return pl.pallas_call(
        forward_counts_kernel,
        out_shape=jax.ShapeDtypeStruct((TILE, PIECES * PARITY_ROWS), bf16),
        name="forward_counts",
    )(keys)


def backward_counts_kernel(core_ref, *refs):
    pieces, out_ref = refs[:PIECES], refs[PIECES]
    core = core_ref[0]
    for p in range(PIECES):
        wanted = 2 - p // 2
        for y in range(RUN):
            head = pieces[p][y, TILE : TILE + KEY_ROWS, :].astype(f32).astype(jnp.int32)
            targets = []
            for half in range(2):
                block = head[:, half * 128 : half * 128 + 128] - (8 * wanted + core)
                cell = head[:, 256 + half * 128 : 384 + half * 128]
                valid = jnp.logical_and(
                    jnp.logical_and(block >= 0, block < 8), jnp.bitwise_and(block, 1) == 0
                )
                found = lax.shift_right_arithmetic(block, 1) * TILE + cell
                targets.append(jnp.where(valid, found, -1))
            lane = (p * RUN + y) * 128
            for step in range(PARITY_ROWS // 16):
                rows = lax.broadcasted_iota(jnp.int32, (16, 128), 0) + step * 16
                total = jnp.zeros((16, 128), f32)
                for e in range(KNN):
                    key = targets[e // 8][e % 8 : e % 8 + 1, :]
                    total = total + jnp.where(key == rows, 1.0, 0.0)
                out_ref[step * 16 : step * 16 + 16, lane : lane + 128] = total.astype(bf16)


def backward_counts(core, pieces):
    return pl.pallas_call(
        backward_counts_kernel,
        in_specs=[pl.BlockSpec(memory_space=pltpu.SMEM)]
        + [pl.BlockSpec(memory_space=pltpu.VMEM)] * PIECES,
        out_shape=jax.ShapeDtypeStruct((PARITY_ROWS, PIECES * PARITY_ROWS), bf16),
        name="backward_counts",
    )(core, *pieces)


def forward_kernel(counts_ref, own_ref, degree_ref, bias_ref, up_ref, *refs):
    pieces, (hidden_ref, scaled_ref, bias_out_ref) = refs[:PIECES], refs[PIECES:]
    total = own_ref[...].astype(f32)
    for p in range(PIECES):
        for y in range(RUN):
            lane = (p * RUN + y) * 128
            total = total + jnp.dot(
                counts_ref[:, lane : lane + 128],
                pieces[p][y, :TILE, :],
                preferred_element_type=f32,
            )
    degree = degree_ref[...]
    pre = total / degree + bias_ref[...]
    sigma = jax.nn.sigmoid(pre)
    hidden_ref[...] = (pre * sigma).astype(bf16)
    grad_pre = up_ref[...].astype(f32) * sigma * (1.0 + pre * (1.0 - sigma))
    scaled_ref[...] = (grad_pre / degree).astype(bf16)
    bias_out_ref[...] = jnp.sum(grad_pre, axis=0, keepdims=True)


def forward_math(counts, own, degree, bias, upstream, pieces):
    return pl.pallas_call(
        forward_kernel,
        out_shape=(
            jax.ShapeDtypeStruct((TILE, HID), bf16),
            jax.ShapeDtypeStruct((TILE, HID), bf16),
            jax.ShapeDtypeStruct((1, HID), f32),
        ),
        name="forward_math",
    )(counts, own, degree, bias, upstream, *pieces)


def backward_kernel(run_ref, counts_ref, feats_ref, bias_ref, *refs):
    pieces, (own_ref, slab_ref, round_ref) = refs[:PIECES], refs[PIECES:]
    total = pieces[2][...].reshape(PARITY_ROWS, HID).astype(f32)
    for p in range(PIECES):
        total = total + jnp.dot(
            counts_ref[:, p * PARITY_ROWS : (p + 1) * PARITY_ROWS],
            pieces[p][...].reshape(PARITY_ROWS, HID),
            preferred_element_type=f32,
        )
    rounded = total.astype(bf16)
    round_ref[...] = rounded.reshape(RUN, TILE, HID)
    own_ref[...] = round_ref[run_ref[0]]
    part = lax.dot_general(
        feats_ref[...].reshape(PARITY_ROWS, F_RUN),
        rounded,
        (((0,), (0,)), ((), ())),
        preferred_element_type=f32,
    ).astype(bf16)
    for row in range(F_RUN // 16):
        for lane in range(HID // 128):
            slab_ref[row * 4 + lane] = part[row * 16 : row * 16 + 16, lane * 128 : lane * 128 + 128]
    slab_ref[BIAS_SLAB] = bias_ref[...]
    for rest in range(BIAS_SLAB + 1, SLABS):
        slab_ref[rest] = jnp.zeros((16, 128), bf16)


def backward_math(run, counts, feats, bias_rows, pieces):
    return pl.pallas_call(
        backward_kernel,
        in_specs=[pl.BlockSpec(memory_space=pltpu.SMEM)]
        + [pl.BlockSpec(memory_space=pltpu.VMEM)] * (3 + PIECES),
        out_shape=(
            jax.ShapeDtypeStruct((TILE, HID), bf16),
            jax.ShapeDtypeStruct((SLABS, 16, 128), bf16),
        ),
        scratch_shapes=[pltpu.VMEM((RUN, TILE, HID), bf16)],
        name="backward_math",
    )(run, counts, feats, bias_rows, *pieces)


def high_low(value):
    high = lax.reduce_precision(value, 8, 7)
    return jnp.concatenate([high, value - high, jnp.zeros((8, 128), f32)], axis=0).astype(bf16)


def on_device(features, weight, bias, tile_cols, tile_count, nbr_slot, nbr_col, nbr_keep, upstream):
    group = (lax.axis_index("yh") * 4 + lax.axis_index("x")) * 8 + lax.axis_index("z")
    run = lax.axis_index("yl")
    core = lax.axis_index("c")
    block_total = 512
    slot_total = tile_cols.shape[1]

    projected = jnp.dot(features, weight, preferred_element_type=f32).astype(bf16)

    live = nbr_keep * (nbr_slot < tile_count[0]).astype(jnp.int32)
    chosen = jnp.zeros_like(nbr_slot)
    for slot in range(slot_total):
        chosen = chosen + jnp.where(nbr_slot == slot, tile_cols[0, slot], 0)
    position = (chosen - (group - 1) * 8) % block_total
    key_block = jnp.where(live > 0, position, DEAD)
    degree = 1.0 + jnp.sum(live, axis=1, keepdims=True).astype(f32)
    pad = jnp.zeros((1, TILE), bf16)
    block_rows = jnp.concatenate([key_block.T.astype(bf16), pad], axis=0)
    cell_rows = jnp.concatenate([nbr_col.T.astype(bf16), pad], axis=0)
    key_rows = jnp.concatenate(
        [block_rows[:8], block_rows[8:], cell_rows[:8], cell_rows[8:]], axis=1
    )
    reach = position // 8
    member = position % 8
    other = (member % 2 != core).astype(jnp.int32)
    place = (reach * 2 + other) * PARITY_ROWS + (member // 2) * TILE + nbr_col
    counts = forward_counts(jnp.where(live > 0, place, -1))

    packed = jnp.concatenate([projected, key_rows], axis=0)
    first = gather_window(packed)
    feats = lax.all_to_all(features.reshape(TILE, RUN, F_RUN).transpose(1, 0, 2), "yl", 0, 0)
    hidden, scaled, bias_part = forward_math(
        counts, projected, degree, bias[None], upstream, first
    )
    counts_back = backward_counts(core.reshape(1), first)
    second = gather_window(scaled)
    own_round, slabs = backward_math(
        run.reshape(1), counts_back, feats, high_low(bias_part.reshape(4, 128)), second
    )
    reduced = jnp.sum(lax.all_to_all(slabs, WIDE + ("c",), 0, 0).astype(f32), axis=0)
    is_bias = (group * 2 + core) == BIAS_SLAB
    piece = jnp.where(is_bias, high_low(reduced[:4] + reduced[4:8]), reduced.astype(bf16))
    column = spread_to(piece, ("yh", "yl"), 8)
    plane = spread_to(column, ("x", "z"), 32)
    plane_other = swap_core(plane)
    both = jnp.stack([plane, plane_other])
    both = jnp.where(core == 0, both, both[::-1])
    both = both.reshape(2, 4, 8, 2, RUN, 16, 128)
    ordered = both.transpose(4, 3, 1, 2, 0, 5, 6).reshape(RUN, SLABS, 16, 128)
    weight_grad = (
        ordered[:, :BIAS_SLAB]
        .reshape(RUN, F_RUN // 16, 4, 16, 128)
        .transpose(0, 1, 3, 2, 4)
        .reshape(RUN * F_RUN, HID)
    )
    bias_rows = ordered[:, BIAS_SLAB].astype(f32)
    bias_grad = jnp.sum(bias_rows[:, :4] + bias_rows[:, 4:8], axis=0).reshape(HID)
    grad_features = lax.dot_general(
        own_round, weight, (((1,), (1,)), ((), ())), preferred_element_type=f32
    ).astype(bf16)
    return hidden, grad_features, weight_grad, bias_grad


def solution(mesh):
    split = Mesh(mesh.devices.reshape(SIZES), AXES)
    rows = P(AXES, None)
    in_specs = (rows, P(), P(), rows, P(AXES), rows, rows, rows, rows)
    out_specs = (rows, rows, P(), P())
    return jax.shard_map(
        on_device, mesh=split, in_specs=in_specs, out_specs=out_specs, check_vma=False
    )
```

```python
import jax
import jax.numpy as jnp
from jax import lax
from jax.experimental import pallas as pl
from jax.experimental.pallas import tpu as pltpu
from jax.sharding import Mesh
from jax.sharding import PartitionSpec as P

TILE = 128
KNN = 15
HID = 512
AXES = ("yh", "x", "z", "yl", "c")
SIZES = (2, 4, 8, 4, 2)
WIDE = ("yh", "x", "z")
RUN = 4
PARITY_ROWS = RUN * TILE
KEY_ROWS = 8
DEAD = 31
KEYS = 16
PIECES = 6
F_RUN = 448
SLABS = 128
BIAS_SLAB = 112

i32 = jnp.int32
bf16 = jnp.bfloat16
f32 = jnp.float32


EAGER = pl.CostEstimate(flops=4_000_000_000, transcendentals=0, bytes_accessed=8_000_000)
SMEM_SPEC = pl.BlockSpec(memory_space=pltpu.SMEM)
VMEM_SPEC = pl.BlockSpec(memory_space=pltpu.VMEM)


def spread_to(shard, axes, count):
    return lax.all_to_all(jnp.broadcast_to(shard[None], (count,) + shard.shape), axes, 0, 0)


FAR = ((31, 32), (63, 0))


def neighbours(block):
    count = 64
    forward = [(i, (i + 1) % count) for i in range(count) if i % 32 != 31]
    backward = [(target, source) for source, target in forward]
    return lax.ppermute(block, WIDE, forward), lax.ppermute(block, WIDE, backward)


def across(shard):
    pairs = list(FAR) + [(b, a) for a, b in FAR]
    return lax.ppermute(shard, WIDE, pairs)


def across_run(received):
    parts = [received]
    for step in range(1, RUN):
        pairs = []
        for group in (0, 31, 32, 63):
            for run in range(RUN):
                for core in range(2):
                    source = (group * RUN + run) * 2 + core
                    pairs.append((source, (group * RUN + (run ^ step)) * 2 + core))
        parts.append(lax.ppermute(received, AXES, pairs))
    return jnp.stack(parts)


def swap_core(block):
    return lax.ppermute(block, "c", [(0, 1), (1, 0)])


def gather_window(shard, copies, far_low, far_high, work):
    received = across(shard)
    own = lax.all_to_all(copies, "yl", 0, 0)
    low, high = neighbours(own)
    own_other = swap_core(own)
    remote = across_run(received)
    result = work(own)
    low, high, result = lax.optimization_barrier((low, high, result))
    low = jnp.where(far_low, remote, low)
    high = jnp.where(far_high, remote, high)
    return (low, swap_core(low), own, own_other, high, swap_core(high)), result


def project_kernel(ids_ref, count_ref, tiles_ref, slot_ref, col_ref, keep_ref, features_ref, weight_ref,
                   shard_ref, copies_ref, cells_ref, digits_ref, degree_ref):
    group, run, core = ids_ref[0], ids_ref[1], ids_ref[2]
    far_low, far_high = ids_ref[3], ids_ref[4]
    slot = slot_ref[...]
    live = keep_ref[...] * (slot < count_ref[0]).astype(i32)
    position = jnp.zeros_like(slot)
    for k in range(tiles_ref.shape[1]):
        block = tiles_ref[0, k] - (group - 1) * 8
        block = jnp.where(block < 0, block + 512, block)
        block = jnp.where(block >= 512, block - 512, block)
        position = position + jnp.where(slot == k, block, 0)
    alive = live > 0
    reach = lax.shift_right_logical(position, 3)
    member = jnp.bitwise_and(position, 7)
    other = jnp.bitwise_xor(jnp.bitwise_and(member, 1), core)
    step = lax.shift_right_logical(member, 1)
    twist = jnp.where(reach == 0, far_low * run, jnp.where(reach == 2, far_high * run, 0))
    place = (reach * 2 + other) * RUN + jnp.bitwise_xor(step, twist)
    pad = jnp.zeros((KEYS - KNN, TILE), i32)

    def rows(value):
        return jnp.concatenate([value, pad], axis=0)

    cells_ref[...] = rows(col_ref[...]).T
    digit = lax.shift_left(jnp.ones_like(place), 4 * jnp.bitwise_and(place, 7))
    for third in range(3):
        chosen = jnp.logical_and(alive, lax.shift_right_logical(place, 3) == third)
        digits_ref[third] = rows(jnp.where(chosen, digit, 0)).T
    degree_ref[...] = 1.0 + jnp.sum(rows(live).T.astype(f32), axis=1, keepdims=True)
    blocks = rows(jnp.where(alive, position, DEAD)).astype(f32).astype(bf16)
    cells = rows(col_ref[...]).astype(f32).astype(bf16)
    keys = jnp.concatenate([blocks[:8], blocks[8:], cells[:8], cells[8:]], axis=1)
    projected = jnp.dot(features_ref[...], weight_ref[...], preferred_element_type=f32).astype(bf16)
    shard_ref[:TILE, :] = projected
    shard_ref[TILE:, :] = keys
    for k in range(RUN):
        copies_ref[k, :TILE, :] = projected
        copies_ref[k, TILE:, :] = keys


def project(ids, tile_count, tile_cols, slot, col, keep, features, weight):
    rows = TILE + KEY_ROWS
    return pl.pallas_call(
        project_kernel,
        in_specs=[SMEM_SPEC] * 3 + [VMEM_SPEC] * 5,
        out_shape=(
            jax.ShapeDtypeStruct((rows, HID), bf16),
            jax.ShapeDtypeStruct((RUN, rows, HID), bf16),
            jax.ShapeDtypeStruct((TILE, KEYS), i32),
            jax.ShapeDtypeStruct((3, TILE, KEYS), i32),
            jax.ShapeDtypeStruct((TILE, 1), f32),
        ),
        name="project",
    )(ids, tile_count, tile_cols, slot, col, keep, features, weight)


def forward_counts_kernel(cells_ref, digits_ref, features_ref, out_ref, feats_ref):
    def rows(step, carry):
        here = pl.ds(step * 16, 16)
        lanes = lax.broadcasted_iota(i32, (16, 128), 1)
        cells = cells_ref[here, :]
        digits = [digits_ref[third, here, :] for third in range(3)]
        totals = [jnp.zeros((16, 128), i32) for _ in range(3)]
        for e in range(KNN):
            hit = cells[:, e : e + 1] == lanes
            for third in range(3):
                totals[third] = totals[third] + jnp.where(hit, digits[third][:, e : e + 1], 0)
        for tile in range(PIECES * RUN):
            digit = lax.shift_right_logical(totals[tile // 8], 4 * (tile % 8))
            count = jnp.bitwise_and(digit, 15).astype(f32).astype(bf16)
            out_ref[here, tile * 128 : (tile + 1) * 128] = count
        return carry

    lax.fori_loop(0, TILE // 16, rows, 0)
    for k in range(RUN):
        feats_ref[k] = features_ref[:, k * F_RUN : (k + 1) * F_RUN]


def forward_counts(cells, digits, features):
    return pl.pallas_call(
        forward_counts_kernel,
        in_specs=[VMEM_SPEC] * 3,
        out_shape=(
            jax.ShapeDtypeStruct((TILE, PIECES * PARITY_ROWS), bf16),
            jax.ShapeDtypeStruct((RUN, TILE, F_RUN), bf16),
        ),
        cost_estimate=EAGER,
        name="forward_counts",
    )(cells, digits, features)


def backward_counts_kernel(core_ref, *refs):
    pieces, out_ref = refs[:PIECES], refs[PIECES]
    core = core_ref[0]
    for p in range(PIECES):
        wanted = 2 - p // 2
        for y in range(RUN):
            head = pieces[p][y, TILE : TILE + KEY_ROWS, :].astype(f32).astype(i32)
            cells, digits = [], []
            for half in range(2):
                block = head[:, half * 128 : half * 128 + 128] - (8 * wanted + core)
                valid = jnp.logical_and(
                    jnp.logical_and(block >= 0, block < 8), jnp.bitwise_and(block, 1) == 0
                )
                shift = 2 * jnp.where(valid, block, 0)
                digits.append(jnp.where(valid, lax.shift_left(jnp.ones_like(shift), shift), 0))
                cells.append(head[:, 256 + half * 128 : 384 + half * 128])
            lane = (p * RUN + y) * 128
            for step in range(TILE // 16):
                rows = lax.broadcasted_iota(i32, (16, 128), 0) + step * 16
                total = jnp.zeros((16, 128), i32)
                for e in range(KNN):
                    cell = cells[e // 8][e % 8 : e % 8 + 1, :]
                    digit = digits[e // 8][e % 8 : e % 8 + 1, :]
                    total = total + jnp.where(cell == rows, digit, 0)
                for k in range(RUN):
                    count = jnp.bitwise_and(lax.shift_right_logical(total, 4 * k), 15)
                    at = k * TILE + step * 16
                    out_ref[at : at + 16, lane : lane + 128] = count.astype(f32).astype(bf16)


def backward_counts(core, pieces):
    return pl.pallas_call(
        backward_counts_kernel,
        in_specs=[SMEM_SPEC] + [VMEM_SPEC] * PIECES,
        out_shape=jax.ShapeDtypeStruct((PARITY_ROWS, PIECES * PARITY_ROWS), bf16),
        cost_estimate=EAGER,
        name="backward_counts",
    )(core, *pieces)


def forward_kernel(counts_ref, shard_ref, degree_ref, bias_ref, up_ref, *refs):
    pieces, (hidden_ref, scaled_ref, copies_ref, bias_out_ref) = refs[:PIECES], refs[PIECES:]
    total = shard_ref[:TILE, :].astype(f32)
    for p in range(PIECES):
        for y in range(RUN):
            lane = (p * RUN + y) * 128
            total = total + jnp.dot(
                counts_ref[:, lane : lane + 128],
                pieces[p][y, :TILE, :],
                preferred_element_type=f32,
            )
    degree = degree_ref[...]
    pre = total / degree + bias_ref[...]
    sigma = jax.nn.sigmoid(pre)
    hidden_ref[...] = (pre * sigma).astype(bf16)
    grad_pre = up_ref[...].astype(f32) * sigma * (1.0 + pre * (1.0 - sigma))
    scaled = (grad_pre / degree).astype(bf16)
    scaled_ref[...] = scaled
    for k in range(RUN):
        copies_ref[k] = scaled
    bias_out_ref[...] = jnp.sum(grad_pre, axis=0, keepdims=True)


def forward_math(counts, shard, degree, bias, upstream, pieces):
    return pl.pallas_call(
        forward_kernel,
        in_specs=[VMEM_SPEC] * (5 + PIECES),
        out_shape=(
            jax.ShapeDtypeStruct((TILE, HID), bf16),
            jax.ShapeDtypeStruct((TILE, HID), bf16),
            jax.ShapeDtypeStruct((RUN, TILE, HID), bf16),
            jax.ShapeDtypeStruct((1, HID), f32),
        ),
        name="forward_math",
    )(counts, shard, degree, bias, upstream, *pieces)


def backward_kernel(run_ref, counts_ref, feats_ref, bias_ref, *refs):
    pieces, (own_ref, slab_ref, round_ref) = refs[:PIECES], refs[PIECES:]
    total = pieces[2][...].reshape(PARITY_ROWS, HID).astype(f32)
    for p in range(PIECES):
        total = total + jnp.dot(
            counts_ref[:, p * PARITY_ROWS : (p + 1) * PARITY_ROWS],
            pieces[p][...].reshape(PARITY_ROWS, HID),
            preferred_element_type=f32,
        )
    rounded = total.astype(bf16)
    round_ref[...] = rounded.reshape(RUN, TILE, HID)
    own_ref[...] = round_ref[run_ref[0]]
    part = lax.dot_general(
        feats_ref[...].reshape(PARITY_ROWS, F_RUN),
        rounded,
        (((0,), (0,)), ((), ())),
        preferred_element_type=f32,
    ).astype(bf16)
    for row in range(F_RUN // 16):
        for lane in range(HID // 128):
            slab_ref[row * 4 + lane] = part[row * 16 : row * 16 + 16, lane * 128 : lane * 128 + 128]
    slab_ref[BIAS_SLAB] = bias_ref[...]
    for rest in range(BIAS_SLAB + 1, SLABS):
        slab_ref[rest] = jnp.zeros((16, 128), bf16)


def backward_math(run, counts, feats, bias_rows, pieces):
    return pl.pallas_call(
        backward_kernel,
        in_specs=[SMEM_SPEC] + [VMEM_SPEC] * (3 + PIECES),
        out_shape=(
            jax.ShapeDtypeStruct((TILE, HID), bf16),
            jax.ShapeDtypeStruct((SLABS, 16, 128), bf16),
        ),
        scratch_shapes=[pltpu.VMEM((RUN, TILE, HID), bf16)],
        name="backward_math",
    )(run, counts, feats, bias_rows, *pieces)


def high_low(value):
    high = lax.reduce_precision(value, 8, 7)
    return jnp.concatenate([high, value - high, jnp.zeros((8, 128), f32)], axis=0).astype(bf16)


def assemble_kernel(core_ref, mine_ref, other_ref, weight_ref, bias_ref):
    first = core_ref[0] == 0
    bias = jnp.zeros((4, 128), f32)
    for plane in range(32):
        x, z = plane // 8, plane % 8
        for column in range(8):
            yh, run = column // 4, column % 4
            mine, other = mine_ref[plane, column], other_ref[plane, column]
            for core in range(2):
                slab = ((yh * 4 + x) * 8 + z) * 2 + core
                if slab > BIAS_SLAB:
                    continue
                keep = first if core == 0 else jnp.logical_not(first)
                value = jnp.where(keep, mine, other)
                if slab == BIAS_SLAB:
                    rows = value.astype(f32)
                    bias = bias + (rows[:4] + rows[4:8])
                    continue
                row, lane = run * F_RUN + (slab // 4) * 16, (slab % 4) * 128
                weight_ref[row : row + 16, lane : lane + 128] = value
    bias_ref[...] = bias


def assemble(core, mine, other):
    return pl.pallas_call(
        assemble_kernel,
        in_specs=[SMEM_SPEC] + [VMEM_SPEC] * 2,
        out_shape=(
            jax.ShapeDtypeStruct((RUN * F_RUN, HID), bf16),
            jax.ShapeDtypeStruct((4, 128), f32),
        ),
        name="assemble",
    )(core, mine, other)


def on_device(features, weight, bias, tile_cols, tile_count, nbr_slot, nbr_col, nbr_keep, upstream):
    group = (lax.axis_index("yh") * 4 + lax.axis_index("x")) * 8 + lax.axis_index("z")
    run = lax.axis_index("yl")
    core = lax.axis_index("c")
    core_id = core.reshape(1).astype(i32)
    far_low = group % 32 == 0
    far_high = group % 32 == 31
    ids = jnp.stack([group, run, core, far_low.astype(i32), far_high.astype(i32)]).astype(i32)

    shard, copies, cells, digits, degree = project(
        ids, tile_count, tile_cols, nbr_slot.T, nbr_col.T, nbr_keep.T, features, weight
    )

    def count_forward(own):
        tied, _ = lax.optimization_barrier((cells, own))
        return forward_counts(tied, digits, features)

    first, (counts, slices) = gather_window(shard, copies, far_low, far_high, count_forward)
    feats = lax.all_to_all(slices, "yl", 0, 0)
    hidden, scaled, scaled_copies, bias_part = forward_math(
        counts, shard, degree, bias[None], upstream, first
    )

    def count_backward(own):
        tied, _ = lax.optimization_barrier((core_id, own))
        return backward_counts(tied, first)

    second, counts_back = gather_window(
        scaled, scaled_copies, far_low, far_high, count_backward
    )
    own_round, slabs = backward_math(
        run.reshape(1), counts_back, feats, high_low(bias_part.reshape(4, 128)), second
    )
    reduced = jnp.sum(lax.all_to_all(slabs, WIDE + ("c",), 0, 0).astype(f32), axis=0)
    is_bias = (group * 2 + core) == BIAS_SLAB
    piece = jnp.where(is_bias, high_low(reduced[:4] + reduced[4:8]), reduced.astype(bf16))
    column = spread_to(piece, ("yh", "yl"), 8)
    plane = spread_to(column, ("x", "z"), 32)
    weight_grad, bias_grad = assemble(core_id, plane, swap_core(plane))
    grad_features = lax.dot_general(
        own_round, weight, (((1,), (1,)), ((), ())), preferred_element_type=f32
    ).astype(bf16)
    return hidden, grad_features, weight_grad, bias_grad.reshape(HID)


def solution(mesh):
    split = Mesh(mesh.devices.reshape(SIZES), AXES)
    rows = P(AXES, None)
    in_specs = (rows, P(), P(), rows, P(AXES), rows, rows, rows, rows)
    out_specs = (rows, rows, P(), P())
    return jax.shard_map(
        on_device, mesh=split, in_specs=in_specs, out_specs=out_specs, check_vma=False
    )
```

```python
import jax
import jax.numpy as jnp
from jax import lax
from jax.experimental import pallas as pl
from jax.experimental.pallas import tpu as pltpu
from jax.sharding import Mesh
from jax.sharding import PartitionSpec as P

TILE = 128
KNN = 15
KEYS = 16
HID = 512
HALF = 256
AXES = ("yh", "x", "z", "yl", "c")
SIZES = (2, 4, 8, 4, 2)
WIDE = ("yh", "x", "z")
GROUPS = 64
RUN = 4
MEMBERS = 8
REACH = 3
WINDOW = REACH * MEMBERS * TILE
BLOCKS = 512
DEAD = 31
F_RUN = 448
SLABS = 64
BIAS_SLAB = 56

i32 = jnp.int32
bf16 = jnp.bfloat16
f32 = jnp.float32

EAGER = pl.CostEstimate(flops=4_000_000_000, transcendentals=0, bytes_accessed=8_000_000)
SMEM_SPEC = pl.BlockSpec(memory_space=pltpu.SMEM)
VMEM_SPEC = pl.BlockSpec(memory_space=pltpu.VMEM)


def spread_to(shard, axes, count):
    return lax.all_to_all(jnp.broadcast_to(shard[None], (count,) + shard.shape), axes, 0, 0)


def neighbours(block):
    forward = [(i, (i + 1) % GROUPS) for i in range(GROUPS)]
    backward = [(target, source) for source, target in forward]
    return lax.ppermute(block, WIDE, forward), lax.ppermute(block, WIDE, backward)


def swap_core(block):
    return lax.ppermute(block, "c", [(0, 1), (1, 0)])


def project_kernel(ids_ref, count_ref, tiles_ref, slot_ref, col_ref, keep_ref, features_ref, weight_ref,
                   copies_ref):
    base = (ids_ref[0] - 1) * MEMBERS
    slot = slot_ref[...]
    live = keep_ref[...] * (slot < count_ref[0]).astype(i32)
    position = jnp.zeros_like(slot)
    for k in range(tiles_ref.shape[1]):
        block = tiles_ref[0, k] - base
        block = jnp.where(block < 0, block + BLOCKS, block)
        block = jnp.where(block >= BLOCKS, block - BLOCKS, block)
        position = position + jnp.where(slot == k, block, 0)
    pad = jnp.zeros((KEYS - KNN, TILE), i32)

    def rows(value):
        return jnp.concatenate([value, pad], axis=0)

    dead = rows(1 - live) + lax.broadcasted_iota(i32, (KEYS, TILE), 0) // KNN
    blocks = jnp.where(dead > 0, DEAD, rows(position))
    keys = jnp.concatenate([blocks, rows(col_ref[...])], axis=1).astype(f32).astype(bf16)
    projected = jnp.dot(features_ref[...], weight_ref[...], preferred_element_type=f32).astype(bf16)
    for k in range(MEMBERS):
        half = (k % 2) * HALF
        copies_ref[k, :TILE, :] = projected[:, half : half + HALF]
        copies_ref[k, TILE:, :] = keys


def project(ids, tile_count, tile_cols, slot, col, keep, features, weight):
    return pl.pallas_call(
        project_kernel,
        in_specs=[SMEM_SPEC] * 3 + [VMEM_SPEC] * 5,
        out_shape=jax.ShapeDtypeStruct((MEMBERS, TILE + KEYS, HALF), bf16),
        name="project",
    )(ids, tile_count, tile_cols, slot, col, keep, features, weight)


def digits_of(block, wanted):
    valid = lax.shift_right_arithmetic(block, 3) == wanted
    shift = 4 * jnp.bitwise_and(block, 7)
    return jnp.where(valid, lax.shift_left(jnp.ones_like(shift), shift), 0)


def forward_counts_kernel(ids_ref, own_ref, counts_ref, degree_ref):
    run = ids_ref[1]
    for core in range(2):
        keys = own_ref[run * 2 + core, TILE:, :].astype(f32).astype(i32).T
        block, cells = keys[:TILE, :], keys[TILE:, :]
        live = jnp.where(block < DEAD, 1.0, 0.0)
        degree_ref[core * TILE : core * TILE + TILE, :] = 1.0 + jnp.sum(live, axis=1, keepdims=True)
        digits = [digits_of(block, reach) for reach in range(REACH)]
        lanes = lax.broadcasted_iota(i32, (16, 128), 1)
        for step in range(TILE // 16):
            here = slice(step * 16, step * 16 + 16)
            totals = [jnp.zeros((16, 128), i32) for _ in range(REACH)]
            for e in range(KNN):
                hit = cells[here, e : e + 1] == lanes
                for reach in range(REACH):
                    totals[reach] = totals[reach] + jnp.where(hit, digits[reach][here, e : e + 1], 0)
            row = core * TILE + step * 16
            for tile in range(REACH * MEMBERS):
                digit = lax.shift_right_logical(totals[tile // 8], 4 * (tile % 8))
                count = jnp.bitwise_and(digit, 15).astype(f32).astype(bf16)
                counts_ref[row : row + 16, tile * 128 : tile * 128 + 128] = count


def forward_counts(ids, own):
    return pl.pallas_call(
        forward_counts_kernel,
        in_specs=[SMEM_SPEC, VMEM_SPEC],
        out_shape=(
            jax.ShapeDtypeStruct((2 * TILE, WINDOW), bf16),
            jax.ShapeDtypeStruct((2 * TILE, 1), f32),
        ),
        cost_estimate=EAGER,
        name="forward_counts",
    )(ids, own)


def backward_counts_kernel(*refs):
    pieces, out_ref = refs[:REACH], refs[REACH]

    def source(member, carry):
        for reach in range(REACH):
            keys = pieces[reach][member, TILE:, :].astype(f32).astype(i32)
            digits = digits_of(keys[:, :TILE], REACH - 1 - reach)
            cells = keys[:, TILE:]
            lanes = pl.ds(reach * MEMBERS * TILE + member * TILE, TILE)
            for step in range(TILE // 16):
                rows = lax.broadcasted_iota(i32, (16, 128), 0) + step * 16
                total = jnp.zeros((16, 128), i32)
                for e in range(KNN):
                    total = total + jnp.where(cells[e : e + 1, :] == rows, digits[e : e + 1, :], 0)
                for k in range(MEMBERS):
                    count = jnp.bitwise_and(lax.shift_right_logical(total, 4 * k), 15)
                    at = k * TILE + step * 16
                    out_ref[at : at + 16, lanes] = count.astype(f32).astype(bf16)
        return carry

    lax.fori_loop(0, MEMBERS, source, 0)


def backward_counts(pieces):
    return pl.pallas_call(
        backward_counts_kernel,
        in_specs=[VMEM_SPEC] * REACH,
        out_shape=jax.ShapeDtypeStruct((MEMBERS * TILE, WINDOW), bf16),
        cost_estimate=EAGER,
        name="backward_counts",
    )(*pieces)


def forward_kernel(ids_ref, counts_ref, degree_ref, bias_ref, up_ref, *refs):
    pieces, (hidden_ref, copies_ref, bias_out_ref) = refs[:REACH], refs[REACH:]
    run = ids_ref[1]
    total = jnp.concatenate(
        [pieces[1][run * 2 + core, :TILE, :].astype(f32) for core in range(2)], axis=0
    )
    for reach in range(REACH):
        for member in range(MEMBERS):
            lane = (reach * MEMBERS + member) * TILE
            total = total + jnp.dot(
                counts_ref[:, lane : lane + TILE],
                pieces[reach][member, :TILE, :],
                preferred_element_type=f32,
            )
    degree = degree_ref[...]
    pre = total / degree + bias_ref[...]
    sigma = jax.nn.sigmoid(pre)
    hidden_ref[...] = (pre * sigma).astype(bf16)
    grad_pre = up_ref[...].astype(f32) * sigma * (1.0 + pre * (1.0 - sigma))
    scaled = (grad_pre / degree).astype(bf16)
    for k in range(RUN):
        copies_ref[k] = scaled
    bias_out_ref[...] = jnp.sum(grad_pre, axis=0, keepdims=True)


def forward_math(ids, counts, degree, bias, upstream, pieces):
    return pl.pallas_call(
        forward_kernel,
        in_specs=[SMEM_SPEC] + [VMEM_SPEC] * (4 + REACH),
        out_shape=(
            jax.ShapeDtypeStruct((2 * TILE, HALF), bf16),
            jax.ShapeDtypeStruct((RUN, 2 * TILE, HALF), bf16),
            jax.ShapeDtypeStruct((1, HALF), f32),
        ),
        name="forward_math",
    )(ids, counts, degree, bias, upstream, *pieces)


def backward_kernel(ids_ref, counts_ref, bias_ref, feats_ref, feats_other_ref, *refs):
    pieces, (own_ref, slab_ref, round_ref) = refs[:REACH], refs[REACH:]
    run, core = ids_ref[1], ids_ref[2]
    group = MEMBERS * TILE
    total = pieces[1][...].reshape(group, HALF).astype(f32)
    for reach in range(REACH):
        total = total + jnp.dot(
            counts_ref[:, reach * group : reach * group + group],
            pieces[reach][...].reshape(group, HALF),
            preferred_element_type=f32,
        )
    round_ref[...] = total.astype(bf16).reshape(MEMBERS, TILE, HALF)
    for k in range(2):
        own_ref[k] = round_ref[run * 2 + k]
    part = jnp.zeros((F_RUN, HALF), f32)
    for feats, side in ((feats_ref, core), (feats_other_ref, 1 - core)):
        rows = jnp.concatenate([round_ref[k * 2 + side] for k in range(RUN)], axis=0)
        part = part + lax.dot_general(
            feats[...].reshape(RUN * TILE, F_RUN),
            rows,
            (((0,), (0,)), ((), ())),
            preferred_element_type=f32,
        )
    part = part.astype(bf16)
    for row in range(F_RUN // 16):
        for lane in range(2):
            slab_ref[row * 2 + lane] = part[row * 16 : row * 16 + 16, lane * 128 : lane * 128 + 128]
    slab_ref[BIAS_SLAB] = bias_ref[...]
    for rest in range(BIAS_SLAB + 1, SLABS):
        slab_ref[rest] = jnp.zeros((16, 128), bf16)


def backward_math(ids, counts, bias_rows, feats, feats_other, pieces):
    return pl.pallas_call(
        backward_kernel,
        in_specs=[SMEM_SPEC] + [VMEM_SPEC] * (4 + REACH),
        out_shape=(
            jax.ShapeDtypeStruct((2, TILE, HALF), bf16),
            jax.ShapeDtypeStruct((SLABS, 16, 128), bf16),
        ),
        scratch_shapes=[pltpu.VMEM((MEMBERS, TILE, HALF), bf16)],
        name="backward_math",
    )(ids, counts, bias_rows, feats, feats_other, *pieces)


def assemble_kernel(ids_ref, mine_ref, other_ref, weight_ref, bias_ref):
    first = ids_ref[2] == 0
    bias = [jnp.zeros((2, 128), f32), jnp.zeros((2, 128), f32)]
    for x in range(4):
        for column in range(64):
            yh, run, z = column // 32, (column // 8) % 4, column % 8
            slab = (yh * 4 + x) * 8 + z
            if slab > BIAS_SLAB:
                continue
            mine, other = mine_ref[x, column], other_ref[x, column]
            for core in range(2):
                keep = first if core == 0 else jnp.logical_not(first)
                value = jnp.where(keep, mine, other)
                if slab == BIAS_SLAB:
                    rows = value.astype(f32)
                    bias[core] = bias[core] + (rows[:2] + rows[2:4])
                else:
                    row, lane = run * F_RUN + (slab // 2) * 16, core * HALF + (slab % 2) * 128
                    weight_ref[row : row + 16, lane : lane + 128] = value
    bias_ref[:2, :] = bias[0]
    bias_ref[2:, :] = bias[1]


def assemble(ids, mine, other):
    return pl.pallas_call(
        assemble_kernel,
        in_specs=[SMEM_SPEC] + [VMEM_SPEC] * 2,
        out_shape=(
            jax.ShapeDtypeStruct((RUN * F_RUN, HID), bf16),
            jax.ShapeDtypeStruct((4, 128), f32),
        ),
        name="assemble",
    )(ids, mine, other)


def high_low(value):
    high = lax.reduce_precision(value, 8, 7)
    return jnp.concatenate([high, value - high, jnp.zeros((12, 128), f32)], axis=0).astype(bf16)


def on_device(features, weight, bias, tile_cols, tile_count, nbr_slot, nbr_col, nbr_keep, upstream):
    group = (lax.axis_index("yh") * 4 + lax.axis_index("x")) * 8 + lax.axis_index("z")
    core = lax.axis_index("c")
    ids = jnp.stack([group, lax.axis_index("yl"), core]).astype(i32)

    copies = project(
        ids, tile_count, tile_cols, nbr_slot.T, nbr_col.T, nbr_keep.T, features, weight
    )
    own = lax.all_to_all(copies, ("yl", "c"), 0, 0)
    up_halves = jnp.stack([upstream[:, :HALF], upstream[:, HALF:]])
    up_halves = lax.all_to_all(up_halves, "c", 0, 0).reshape(2 * TILE, HALF)
    low, high = neighbours(own)
    counts, degree = forward_counts(ids, own)
    low, high, counts, degree, up_halves = lax.optimization_barrier(
        (low, high, counts, degree, up_halves)
    )
    first = (low, own, high)
    slices = jnp.stack([features[:, k * F_RUN : (k + 1) * F_RUN] for k in range(RUN)])
    feats = lax.all_to_all(slices, "yl", 0, 0)
    feats_other = swap_core(feats)
    bias_half = lax.dynamic_slice(bias, (core * HALF,), (HALF,))[None]
    hidden_halves, scaled, bias_part = forward_math(
        ids, counts, degree, bias_half, up_halves, first
    )
    own = lax.all_to_all(scaled, "yl", 0, 0)
    counts_back = backward_counts(first)
    low, high = neighbours(own)
    rounds, slabs = backward_math(
        ids, counts_back, high_low(bias_part.reshape(2, 128)), feats, feats_other,
        tuple(block.reshape(MEMBERS, TILE, HALF) for block in (low, own, high)),
    )
    reduced = jnp.sum(lax.all_to_all(slabs, WIDE, 0, 0).astype(f32), axis=0)
    piece = jnp.where(
        group == BIAS_SLAB, high_low(reduced[:2] + reduced[2:4]), reduced.astype(bf16)
    )
    column = spread_to(piece, ("yh", "yl", "z"), 64)
    plane = spread_to(column, "x", 4)
    weight_grad, bias_grad = assemble(ids, plane, swap_core(plane))
    rows = jnp.concatenate([hidden_halves.reshape(2, TILE, HALF), rounds], axis=1)
    rows = lax.all_to_all(rows, "c", 0, 0)
    hidden = jnp.concatenate([rows[0, :TILE], rows[1, :TILE]], axis=1)
    own_round = jnp.concatenate([rows[0, TILE:], rows[1, TILE:]], axis=1)
    grad_features = lax.dot_general(
        own_round, weight, (((1,), (1,)), ((), ())), preferred_element_type=f32
    ).astype(bf16)
    return hidden, grad_features, weight_grad, bias_grad.reshape(HID)


def solution(mesh):
    split = Mesh(mesh.devices.reshape(SIZES), AXES)
    rows = P(AXES, None)
    in_specs = (rows, P(), P(), rows, P(AXES), rows, rows, rows, rows)
    out_specs = (rows, rows, P(), P())
    return jax.shard_map(
        on_device, mesh=split, in_specs=in_specs, out_specs=out_specs, check_vma=False
    )
```

```python
import jax
import jax.numpy as jnp
from jax import lax
from jax.experimental import pallas as pl
from jax.experimental.pallas import tpu as pltpu
from jax.sharding import Mesh
from jax.sharding import PartitionSpec as P

TILE = 128
KNN = 15
KEYS = 16
HID = 512
HALF = 256
AXES = ("yh", "x", "z", "yl", "c")
SIZES = (2, 4, 8, 4, 2)
WIDE = ("yh", "x", "z")
GROUPS = 64
RUN = 4
MEMBERS = 8
REACH = 3
PIECES = 7
WINDOW = REACH * MEMBERS * TILE
BLOCKS = 512
DEAD = 31
F_RUN = 448
SLABS = 64
BIAS_SLAB = 56

i32 = jnp.int32
bf16 = jnp.bfloat16
f32 = jnp.float32

EAGER = pl.CostEstimate(flops=4_000_000_000, transcendentals=0, bytes_accessed=8_000_000)
SMEM_SPEC = pl.BlockSpec(memory_space=pltpu.SMEM)
VMEM_SPEC = pl.BlockSpec(memory_space=pltpu.VMEM)


def spread_to(shard, axes, count):
    return lax.all_to_all(jnp.broadcast_to(shard[None], (count,) + shard.shape), axes, 0, 0)


FAR = ((31, 32), (63, 0), (32, 31), (0, 63))


def device(group, run, core):
    return (group * RUN + run) * 2 + core


def across(same, cross):
    pairs = [(a, b, r, c) for a, b in FAR for r in range(RUN) for c in range(2)]
    straight = [(device(a, r, c), device(b, r, c)) for a, b, r, c in pairs]
    turned = [(device(a, r, c), device(b, r, 1 - c)) for a, b, r, c in pairs]
    got = lax.ppermute(same, AXES, straight)
    return got if cross is None else (got, lax.ppermute(cross, AXES, turned))


def along_run(block):
    parts = [block]
    for step in range(1, RUN):
        pairs = [
            (device(a, r, c), device(a, r ^ step, c))
            for a, _ in FAR for r in range(RUN) for c in range(2)
        ]
        parts.append(lax.ppermute(block, AXES, pairs))
    return tuple(parts)


def block_of(ids_ref, pieces, reach, member):
    own, low, high = pieces[:REACH]
    if reach == 1:
        return own[member, :TILE, :]
    near = (low, high)[reach // 2][member, :TILE, :]
    far = pieces[REACH + member // 2][member % 2, :TILE, :]
    return jnp.where(ids_ref[3 + reach // 2] > 0, far, near)


def keys_of(ids_ref, pieces, reach, member):
    own, low, high = pieces[:REACH]
    if reach == 1:
        return own[member, TILE:, :].astype(f32)
    near = (low, high)[reach // 2][member, TILE:, :].astype(f32)
    far = pieces[REACH + member // 2][member % 2, TILE:, :].astype(f32)
    return jnp.where(ids_ref[3 + reach // 2] > 0, far, near)


def neighbours(block):
    forward = [(i, (i + 1) % GROUPS) for i in range(GROUPS) if i % 32 != 31]
    backward = [(target, source) for source, target in forward]
    return lax.ppermute(block, WIDE, forward), lax.ppermute(block, WIDE, backward)


def swap_core(block):
    return lax.ppermute(block, "c", [(0, 1), (1, 0)])


def project_kernel(ids_ref, count_ref, tiles_ref, slot_ref, col_ref, keep_ref, features_ref, weight_ref,
                   copies_ref, same_ref, cross_ref):
    base = (ids_ref[0] - 1) * MEMBERS
    slot = slot_ref[...]
    live = keep_ref[...] * (slot < count_ref[0]).astype(i32)
    position = jnp.zeros_like(slot)
    for k in range(tiles_ref.shape[1]):
        block = tiles_ref[0, k] - base
        block = jnp.where(block < 0, block + BLOCKS, block)
        block = jnp.where(block >= BLOCKS, block - BLOCKS, block)
        position = position + jnp.where(slot == k, block, 0)
    pad = jnp.zeros((KEYS - KNN, TILE), i32)

    def rows(value):
        return jnp.concatenate([value, pad], axis=0)

    dead = rows(1 - live) + lax.broadcasted_iota(i32, (KEYS, TILE), 0) // KNN
    blocks = jnp.where(dead > 0, DEAD, rows(position))
    keys = jnp.concatenate([blocks, rows(col_ref[...])], axis=1).astype(f32).astype(bf16)
    projected = jnp.dot(features_ref[...], weight_ref[...], preferred_element_type=f32).astype(bf16)
    for k in range(MEMBERS):
        half = (k % 2) * HALF
        copies_ref[k, :TILE, :] = projected[:, half : half + HALF]
        copies_ref[k, TILE:, :] = keys
    first = ids_ref[2] == 0
    left, right = projected[:, :HALF], projected[:, HALF:]
    same_ref[:TILE, :] = jnp.where(first, left, right)
    same_ref[TILE:, :] = keys
    cross_ref[:TILE, :] = jnp.where(first, right, left)
    cross_ref[TILE:, :] = keys


def project(ids, tile_count, tile_cols, slot, col, keep, features, weight):
    return pl.pallas_call(
        project_kernel,
        in_specs=[SMEM_SPEC] * 3 + [VMEM_SPEC] * 5,
        out_shape=(
            jax.ShapeDtypeStruct((MEMBERS, TILE + KEYS, HALF), bf16),
            jax.ShapeDtypeStruct((TILE + KEYS, HALF), bf16),
            jax.ShapeDtypeStruct((TILE + KEYS, HALF), bf16),
        ),
        name="project",
    )(ids, tile_count, tile_cols, slot, col, keep, features, weight)


def digits_of(block, wanted):
    valid = lax.shift_right_arithmetic(block, 3) == wanted
    shift = 4 * jnp.bitwise_and(block, 7)
    return jnp.where(valid, lax.shift_left(jnp.ones_like(shift), shift), 0)


def forward_counts_kernel(ids_ref, own_ref, counts_ref, degree_ref):
    run = ids_ref[1]
    for core in range(2):
        keys = own_ref[run * 2 + core, TILE:, :].astype(f32).astype(i32).T
        block, cells = keys[:TILE, :], keys[TILE:, :]
        live = jnp.where(block < DEAD, 1.0, 0.0)
        degree_ref[core * TILE : core * TILE + TILE, :] = 1.0 + jnp.sum(live, axis=1, keepdims=True)
        reach_of = lax.shift_right_logical(block, 3)
        low_twist = jnp.where(reach_of == 0, ids_ref[3] * run * 2, 0)
        twist = low_twist + jnp.where(reach_of == 2, ids_ref[4] * run * 2, 0)
        block = jnp.bitwise_xor(block, twist)
        digits = [digits_of(block, reach) for reach in range(REACH)]
        lanes = lax.broadcasted_iota(i32, (16, 128), 1)
        for step in range(TILE // 16):
            here = slice(step * 16, step * 16 + 16)
            totals = [jnp.zeros((16, 128), i32) for _ in range(REACH)]
            for e in range(KNN):
                hit = cells[here, e : e + 1] == lanes
                for reach in range(REACH):
                    totals[reach] = totals[reach] + jnp.where(hit, digits[reach][here, e : e + 1], 0)
            row = core * TILE + step * 16
            for tile in range(REACH * MEMBERS):
                digit = lax.shift_right_logical(totals[tile // 8], 4 * (tile % 8))
                count = jnp.bitwise_and(digit, 15).astype(f32).astype(bf16)
                counts_ref[row : row + 16, tile * 128 : tile * 128 + 128] = count


def forward_counts(ids, own):
    return pl.pallas_call(
        forward_counts_kernel,
        in_specs=[SMEM_SPEC, VMEM_SPEC],
        out_shape=(
            jax.ShapeDtypeStruct((2 * TILE, WINDOW), bf16),
            jax.ShapeDtypeStruct((2 * TILE, 1), f32),
        ),
        cost_estimate=EAGER,
        name="forward_counts",
    )(ids, own)


def backward_counts_kernel(ids_ref, *refs):
    pieces, out_ref = refs[:PIECES], refs[PIECES]
    for member in range(MEMBERS):
        for reach in range(REACH):
            keys = keys_of(ids_ref, pieces, reach, member).astype(i32)
            digits = digits_of(keys[:, :TILE], REACH - 1 - reach)
            cells = keys[:, TILE:]
            lane = (reach * MEMBERS + member) * TILE
            for step in range(TILE // 16):
                rows = lax.broadcasted_iota(i32, (16, 128), 0) + step * 16
                total = jnp.zeros((16, 128), i32)
                for e in range(KNN):
                    total = total + jnp.where(cells[e : e + 1, :] == rows, digits[e : e + 1, :], 0)
                for k in range(MEMBERS):
                    count = jnp.bitwise_and(lax.shift_right_logical(total, 4 * k), 15)
                    at = k * TILE + step * 16
                    out_ref[at : at + 16, lane : lane + TILE] = count.astype(f32).astype(bf16)


def backward_counts(ids, pieces):
    return pl.pallas_call(
        backward_counts_kernel,
        in_specs=[SMEM_SPEC] + [VMEM_SPEC] * PIECES,
        out_shape=jax.ShapeDtypeStruct((MEMBERS * TILE, WINDOW), bf16),
        cost_estimate=EAGER,
        name="backward_counts",
    )(ids, *pieces)


def forward_kernel(ids_ref, counts_ref, degree_ref, bias_ref, up_ref, up_other_ref, *refs):
    pieces = refs[:PIECES]
    hidden_ref, hidden_other_ref, copies_ref, scaled_ref, bias_out_ref = refs[PIECES:]
    run, first = ids_ref[1], ids_ref[2] == 0
    total = jnp.concatenate(
        [pieces[0][run * 2 + core, :TILE, :].astype(f32) for core in range(2)], axis=0
    )
    for reach in range(REACH):
        for member in range(MEMBERS):
            lane = (reach * MEMBERS + member) * TILE
            total = total + jnp.dot(
                counts_ref[:, lane : lane + TILE],
                block_of(ids_ref, pieces, reach, member),
                preferred_element_type=f32,
            )
    degree = degree_ref[...]
    pre = total / degree + bias_ref[...]
    sigma = jax.nn.sigmoid(pre)
    hidden = (pre * sigma).astype(bf16)
    hidden_ref[...] = jnp.where(first, hidden[:TILE], hidden[TILE:])
    hidden_other_ref[...] = jnp.where(first, hidden[TILE:], hidden[:TILE])
    up_mine = jnp.where(first, up_ref[:, :HALF], up_ref[:, HALF:])
    up_other = up_other_ref[...]
    up = jnp.concatenate(
        [jnp.where(first, up_mine, up_other), jnp.where(first, up_other, up_mine)], axis=0
    )
    grad_pre = up.astype(f32) * sigma * (1.0 + pre * (1.0 - sigma))
    scaled = (grad_pre / degree).astype(bf16).reshape(2, TILE, HALF)
    scaled_ref[...] = scaled
    for k in range(RUN):
        copies_ref[k] = scaled
    bias_out_ref[...] = jnp.sum(grad_pre, axis=0, keepdims=True)


def forward_math(ids, counts, degree, bias, upstream, up_other, pieces):
    return pl.pallas_call(
        forward_kernel,
        in_specs=[SMEM_SPEC] + [VMEM_SPEC] * (5 + PIECES),
        out_shape=(
            jax.ShapeDtypeStruct((TILE, HALF), bf16),
            jax.ShapeDtypeStruct((TILE, HALF), bf16),
            jax.ShapeDtypeStruct((RUN, 2, TILE, HALF), bf16),
            jax.ShapeDtypeStruct((2, TILE, HALF), bf16),
            jax.ShapeDtypeStruct((1, HALF), f32),
        ),
        name="forward_math",
    )(ids, counts, degree, bias, upstream, up_other, *pieces)


def backward_kernel(ids_ref, counts_ref, bias_ref, feats_ref, feats_other_ref, *refs):
    pieces, (own_ref, other_ref, slab_ref, round_ref) = refs[:PIECES], refs[PIECES:]
    run, core = ids_ref[1], ids_ref[2]
    group = MEMBERS * TILE
    total = pieces[0][...].reshape(group, HALF).astype(f32)
    for reach in range(REACH):
        rows = [block_of(ids_ref, pieces, reach, member) for member in range(MEMBERS)]
        total = total + jnp.dot(
            counts_ref[:, reach * group : reach * group + group],
            jnp.concatenate(rows, axis=0),
            preferred_element_type=f32,
        )
    round_ref[...] = total.astype(bf16).reshape(MEMBERS, TILE, HALF)
    own_ref[...] = round_ref[run * 2 + core]
    other_ref[...] = round_ref[run * 2 + 1 - core]
    part = jnp.zeros((F_RUN, HALF), f32)
    for feats, side in ((feats_ref, core), (feats_other_ref, 1 - core)):
        rows = jnp.concatenate([round_ref[k * 2 + side] for k in range(RUN)], axis=0)
        part = part + lax.dot_general(
            feats[...].reshape(RUN * TILE, F_RUN),
            rows,
            (((0,), (0,)), ((), ())),
            preferred_element_type=f32,
        )
    part = part.astype(bf16)
    for row in range(F_RUN // 16):
        for lane in range(2):
            slab_ref[row * 2 + lane] = part[row * 16 : row * 16 + 16, lane * 128 : lane * 128 + 128]
    slab_ref[BIAS_SLAB] = bias_ref[...]
    for rest in range(BIAS_SLAB + 1, SLABS):
        slab_ref[rest] = jnp.zeros((16, 128), bf16)


def backward_math(ids, counts, bias_rows, feats, feats_other, pieces):
    return pl.pallas_call(
        backward_kernel,
        in_specs=[SMEM_SPEC] + [VMEM_SPEC] * (4 + PIECES),
        out_shape=(
            jax.ShapeDtypeStruct((TILE, HALF), bf16),
            jax.ShapeDtypeStruct((TILE, HALF), bf16),
            jax.ShapeDtypeStruct((SLABS, 16, 128), bf16),
        ),
        scratch_shapes=[pltpu.VMEM((MEMBERS, TILE, HALF), bf16)],
        name="backward_math",
    )(ids, counts, bias_rows, feats, feats_other, *pieces)


def assemble_kernel(ids_ref, mine_ref, other_ref, weight_ref, bias_ref):
    first = ids_ref[2] == 0
    bias = [jnp.zeros((2, 128), f32), jnp.zeros((2, 128), f32)]
    for x in range(4):
        for column in range(64):
            yh, run, z = column // 32, (column // 8) % 4, column % 8
            slab = (yh * 4 + x) * 8 + z
            if slab > BIAS_SLAB:
                continue
            mine, other = mine_ref[x, column], other_ref[x, column]
            for core in range(2):
                keep = first if core == 0 else jnp.logical_not(first)
                value = jnp.where(keep, mine, other)
                if slab == BIAS_SLAB:
                    rows = value.astype(f32)
                    bias[core] = bias[core] + (rows[:2] + rows[2:4])
                else:
                    row, lane = run * F_RUN + (slab // 2) * 16, core * HALF + (slab % 2) * 128
                    weight_ref[row : row + 16, lane : lane + 128] = value
    bias_ref[:2, :] = bias[0]
    bias_ref[2:, :] = bias[1]


def assemble(ids, mine, other):
    return pl.pallas_call(
        assemble_kernel,
        in_specs=[SMEM_SPEC] + [VMEM_SPEC] * 2,
        out_shape=(
            jax.ShapeDtypeStruct((RUN * F_RUN, HID), bf16),
            jax.ShapeDtypeStruct((4, 128), f32),
        ),
        name="assemble",
    )(ids, mine, other)


def high_low(value):
    high = lax.reduce_precision(value, 8, 7)
    return jnp.concatenate([high, value - high, jnp.zeros((12, 128), f32)], axis=0).astype(bf16)


def on_device(features, weight, bias, tile_cols, tile_count, nbr_slot, nbr_col, nbr_keep, upstream):
    group = (lax.axis_index("yh") * 4 + lax.axis_index("x")) * 8 + lax.axis_index("z")
    core = lax.axis_index("c")
    first = core == 0
    far_low, far_high = group % 32 == 0, group % 32 == 31
    ids = jnp.stack([group, lax.axis_index("yl"), core, far_low, far_high]).astype(i32)

    copies, same, cross = project(
        ids, tile_count, tile_cols, nbr_slot.T, nbr_col.T, nbr_keep.T, features, weight
    )
    straight, turned = across(same, cross)
    own = lax.all_to_all(copies, ("yl", "c"), 0, 0)
    tied, _ = lax.optimization_barrier((upstream, copies))
    up_other = swap_core(jnp.where(first, tied[:, HALF:], tied[:, :HALF]))
    slices = jnp.stack([features[:, k * F_RUN : (k + 1) * F_RUN] for k in range(RUN)])
    straight, turned, own, up_other, slices = lax.optimization_barrier(
        (straight, turned, own, up_other, slices)
    )
    received = jnp.stack([jnp.where(first, straight, turned), jnp.where(first, turned, straight)])
    low, high = neighbours(own)
    parts = along_run(received)
    counts, degree = forward_counts(ids, own)
    feats = lax.all_to_all(slices, "yl", 0, 0)
    feats_other = swap_core(feats)
    pieces = (own, low, high) + parts
    bias_half = jnp.where(first, bias[:HALF], bias[HALF:])[None]
    hidden_mine, hidden_send, scaled_copies, scaled, bias_part = forward_math(
        ids, counts, degree, bias_half, upstream, up_other, pieces
    )

    received = across(scaled, None)
    own = lax.all_to_all(scaled_copies, "yl", 0, 0)
    hidden_got = swap_core(hidden_send)
    counts_back = backward_counts(ids, pieces)
    received, own, counts_back = lax.optimization_barrier((received, own, counts_back))
    own = own.reshape(MEMBERS, TILE, HALF)
    low, high = neighbours(own)
    parts = along_run(received)
    round_mine, round_send, slabs = backward_math(
        ids, counts_back, high_low(bias_part.reshape(2, 128)), feats, feats_other,
        (own, low, high) + parts,
    )
    round_got = swap_core(round_send)
    own_round = jnp.where(
        first,
        jnp.concatenate([round_mine, round_got], axis=1),
        jnp.concatenate([round_got, round_mine], axis=1),
    )
    grad_features = lax.dot_general(
        own_round, weight, (((1,), (1,)), ((), ())), preferred_element_type=f32
    ).astype(bf16)
    hidden = jnp.where(
        first,
        jnp.concatenate([hidden_mine, hidden_got], axis=1),
        jnp.concatenate([hidden_got, hidden_mine], axis=1),
    )
    terms = lax.all_to_all(slabs, WIDE, 0, 0)
    terms, grad_features, hidden = lax.optimization_barrier((terms, grad_features, hidden))
    reduced = jnp.sum(terms.astype(f32), axis=0)
    piece = jnp.where(
        group == BIAS_SLAB, high_low(reduced[:2] + reduced[2:4]), reduced.astype(bf16)
    )
    column = spread_to(piece, ("yh", "yl", "z"), 64)
    plane = spread_to(column, "x", 4)
    weight_grad, bias_grad = assemble(ids, plane, swap_core(plane))
    return hidden, grad_features, weight_grad, bias_grad.reshape(HID)


def solution(mesh):
    split = Mesh(mesh.devices.reshape(SIZES), AXES)
    rows = P(AXES, None)
    in_specs = (rows, P(), P(), rows, P(AXES), rows, rows, rows, rows)
    out_specs = (rows, rows, P(), P())
    return jax.shard_map(
        on_device, mesh=split, in_specs=in_specs, out_specs=out_specs, check_vma=False
    )
```

```python
import jax
import jax.numpy as jnp
from jax import lax
from jax.experimental import pallas as pl
from jax.experimental.pallas import tpu as pltpu
from jax.sharding import Mesh
from jax.sharding import PartitionSpec as P

TILE = 128
KNN = 15
KEYS = 16
HID = 512
HALF = 256
AXES = ("yh", "x", "z", "yl", "c")
SIZES = (2, 4, 8, 4, 2)
WIDE = ("yh", "x", "z")
GROUPS = 64
RUN = 4
MEMBERS = 8
REACH = 3
PIECES = 7
WINDOW = REACH * MEMBERS * TILE
BLOCKS = 512
DEAD = 31
F_RUN = 448
SLABS = 64
BIAS_SLAB = 56

i32 = jnp.int32
bf16 = jnp.bfloat16
f32 = jnp.float32

EAGER = pl.CostEstimate(flops=4_000_000_000, transcendentals=0, bytes_accessed=8_000_000)
SMEM_SPEC = pl.BlockSpec(memory_space=pltpu.SMEM)
VMEM_SPEC = pl.BlockSpec(memory_space=pltpu.VMEM)


def spread_to(shard, axes, count):
    return lax.all_to_all(jnp.broadcast_to(shard[None], (count,) + shard.shape), axes, 0, 0)


FAR = ((31, 32), (63, 0), (32, 31), (0, 63))


def device(group, run, core):
    return (group * RUN + run) * 2 + core


def across(same, cross):
    pairs = [(a, b, r, c) for a, b in FAR for r in range(RUN) for c in range(2)]
    straight = [(device(a, r, c), device(b, r, c)) for a, b, r, c in pairs]
    turned = [(device(a, r, c), device(b, r, 1 - c)) for a, b, r, c in pairs]
    got = lax.ppermute(same, AXES, straight)
    return got if cross is None else (got, lax.ppermute(cross, AXES, turned))


def along_run(block):
    parts = [block]
    for step in range(1, RUN):
        pairs = [
            (device(a, r, c), device(a, r ^ step, c))
            for a, _ in FAR for r in range(RUN) for c in range(2)
        ]
        parts.append(lax.ppermute(block, AXES, pairs))
    return tuple(parts)


def block_of(ids_ref, pieces, reach, member):
    own, low, high = pieces[:REACH]
    if reach == 1:
        return own[member, :TILE, :]
    near = (low, high)[reach // 2][member, :TILE, :]
    far = pieces[REACH + member // 2][member % 2, :TILE, :]
    return jnp.where(ids_ref[3 + reach // 2] > 0, far, near)


def keys_of(ids_ref, pieces, reach, member):
    own, low, high = pieces[:REACH]
    if reach == 1:
        return own[member, TILE:, :].astype(f32)
    near = (low, high)[reach // 2][member, TILE:, :].astype(f32)
    far = pieces[REACH + member // 2][member % 2, TILE:, :].astype(f32)
    return jnp.where(ids_ref[3 + reach // 2] > 0, far, near)


def neighbours(block):
    forward = [(i, (i + 1) % GROUPS) for i in range(GROUPS) if i % 32 != 31]
    backward = [(target, source) for source, target in forward]
    return lax.ppermute(block, WIDE, forward), lax.ppermute(block, WIDE, backward)


def swap_core(block):
    return lax.ppermute(block, "c", [(0, 1), (1, 0)])


def project_kernel(ids_ref, count_ref, tiles_ref, slot_ref, col_ref, keep_ref, features_ref, weight_ref,
                   copies_ref, same_ref, cross_ref):
    base = (ids_ref[0] - 1) * MEMBERS
    slot = slot_ref[...]
    live = keep_ref[...] * (slot < count_ref[0]).astype(i32)
    position = jnp.zeros_like(slot)
    for k in range(tiles_ref.shape[1]):
        block = tiles_ref[0, k] - base
        block = jnp.where(block < 0, block + BLOCKS, block)
        block = jnp.where(block >= BLOCKS, block - BLOCKS, block)
        position = position + jnp.where(slot == k, block, 0)
    pad = jnp.zeros((KEYS - KNN, TILE), i32)

    def rows(value):
        return jnp.concatenate([value, pad], axis=0)

    dead = rows(1 - live) + lax.broadcasted_iota(i32, (KEYS, TILE), 0) // KNN
    blocks = jnp.where(dead > 0, DEAD, rows(position))
    keys = jnp.concatenate([blocks, rows(col_ref[...])], axis=1).astype(f32).astype(bf16)
    projected = jnp.dot(features_ref[...], weight_ref[...], preferred_element_type=f32).astype(bf16)
    for k in range(MEMBERS):
        half = (k % 2) * HALF
        copies_ref[k, :TILE, :] = projected[:, half : half + HALF]
        copies_ref[k, TILE:, :] = keys
    first = ids_ref[2] == 0
    left, right = projected[:, :HALF], projected[:, HALF:]
    same_ref[:TILE, :] = jnp.where(first, left, right)
    same_ref[TILE:, :] = keys
    cross_ref[:TILE, :] = jnp.where(first, right, left)
    cross_ref[TILE:, :] = keys


def project(ids, tile_count, tile_cols, slot, col, keep, features, weight):
    return pl.pallas_call(
        project_kernel,
        in_specs=[SMEM_SPEC] * 3 + [VMEM_SPEC] * 5,
        out_shape=(
            jax.ShapeDtypeStruct((MEMBERS, TILE + KEYS, HALF), bf16),
            jax.ShapeDtypeStruct((TILE + KEYS, HALF), bf16),
            jax.ShapeDtypeStruct((TILE + KEYS, HALF), bf16),
        ),
        name="project",
    )(ids, tile_count, tile_cols, slot, col, keep, features, weight)


def digits_of(block, wanted):
    valid = lax.shift_right_arithmetic(block, 3) == wanted
    shift = 4 * jnp.bitwise_and(block, 7)
    return jnp.where(valid, lax.shift_left(jnp.ones_like(shift), shift), 0)


def forward_counts_kernel(ids_ref, own_ref, counts_ref, degree_ref):
    run = ids_ref[1]
    for core in range(2):
        keys = own_ref[run * 2 + core, TILE:, :].astype(f32).astype(i32).T
        block, cells = keys[:TILE, :], keys[TILE:, :]
        live = jnp.where(block < DEAD, 1.0, 0.0)
        degree_ref[core * TILE : core * TILE + TILE, :] = 1.0 + jnp.sum(live, axis=1, keepdims=True)
        reach_of = lax.shift_right_logical(block, 3)
        low_twist = jnp.where(reach_of == 0, ids_ref[3] * run * 2, 0)
        twist = low_twist + jnp.where(reach_of == 2, ids_ref[4] * run * 2, 0)
        block = jnp.bitwise_xor(block, twist)
        digits = [digits_of(block, reach) for reach in range(REACH)]
        lanes = lax.broadcasted_iota(i32, (16, 128), 1)
        for step in range(TILE // 16):
            here = slice(step * 16, step * 16 + 16)
            totals = [jnp.zeros((16, 128), i32) for _ in range(REACH)]
            for e in range(KNN):
                hit = cells[here, e : e + 1] == lanes
                for reach in range(REACH):
                    totals[reach] = totals[reach] + jnp.where(hit, digits[reach][here, e : e + 1], 0)
            row = core * TILE + step * 16
            for tile in range(REACH * MEMBERS):
                digit = lax.shift_right_logical(totals[tile // 8], 4 * (tile % 8))
                count = jnp.bitwise_and(digit, 15).astype(f32).astype(bf16)
                counts_ref[row : row + 16, tile * 128 : tile * 128 + 128] = count


def forward_counts(ids, own):
    return pl.pallas_call(
        forward_counts_kernel,
        in_specs=[SMEM_SPEC, VMEM_SPEC],
        out_shape=(
            jax.ShapeDtypeStruct((2 * TILE, WINDOW), bf16),
            jax.ShapeDtypeStruct((2 * TILE, 1), f32),
        ),
        cost_estimate=EAGER,
        name="forward_counts",
    )(ids, own)


def backward_counts_kernel(ids_ref, *refs):
    pieces, out_ref = refs[:PIECES], refs[PIECES]
    for member in range(MEMBERS):
        for reach in range(REACH):
            keys = keys_of(ids_ref, pieces, reach, member).astype(i32)
            digits = digits_of(keys[:, :TILE], REACH - 1 - reach)
            cells = keys[:, TILE:]
            lane = (reach * MEMBERS + member) * TILE
            for step in range(TILE // 16):
                rows = lax.broadcasted_iota(i32, (16, 128), 0) + step * 16
                total = jnp.zeros((16, 128), i32)
                for e in range(KNN):
                    total = total + jnp.where(cells[e : e + 1, :] == rows, digits[e : e + 1, :], 0)
                for k in range(MEMBERS):
                    count = jnp.bitwise_and(lax.shift_right_logical(total, 4 * k), 15)
                    at = k * TILE + step * 16
                    out_ref[at : at + 16, lane : lane + TILE] = count.astype(f32).astype(bf16)


def backward_counts(ids, pieces):
    return pl.pallas_call(
        backward_counts_kernel,
        in_specs=[SMEM_SPEC] + [VMEM_SPEC] * PIECES,
        out_shape=jax.ShapeDtypeStruct((MEMBERS * TILE, WINDOW), bf16),
        cost_estimate=EAGER,
        name="backward_counts",
    )(ids, *pieces)


def forward_own_kernel(ids_ref, counts_ref, own_ref, total_ref):
    run = ids_ref[1]
    total = jnp.concatenate(
        [own_ref[run * 2 + core, :TILE, :].astype(f32) for core in range(2)], axis=0
    )
    for member in range(MEMBERS):
        lane = (MEMBERS + member) * TILE
        total = total + jnp.dot(
            counts_ref[:, lane : lane + TILE],
            own_ref[member, :TILE, :],
            preferred_element_type=f32,
        )
    total_ref[...] = total


def forward_own(ids, counts, own):
    return pl.pallas_call(
        forward_own_kernel,
        in_specs=[SMEM_SPEC] + [VMEM_SPEC] * 2,
        out_shape=jax.ShapeDtypeStruct((2 * TILE, HALF), f32),
        cost_estimate=EAGER,
        name="forward_own",
    )(ids, counts, own)


def backward_own_kernel(counts_ref, own_ref, total_ref):
    group = MEMBERS * TILE
    own = own_ref[...].reshape(group, HALF)
    total_ref[...] = own.astype(f32) + jnp.dot(
        counts_ref[:, group : 2 * group], own, preferred_element_type=f32
    )


def backward_own(counts, own):
    return pl.pallas_call(
        backward_own_kernel,
        in_specs=[VMEM_SPEC] * 2,
        out_shape=jax.ShapeDtypeStruct((MEMBERS * TILE, HALF), f32),
        cost_estimate=EAGER,
        name="backward_own",
    )(counts, own)


def forward_kernel(
    ids_ref, counts_ref, total_ref, degree_ref, bias_ref, up_ref, up_other_ref, *refs
):
    pieces = (None,) + refs[: PIECES - 1]
    hidden_ref, hidden_other_ref, copies_ref, scaled_ref, bias_out_ref = refs[PIECES - 1 :]
    first = ids_ref[2] == 0
    total = total_ref[...]
    for reach in (0, 2):
        for member in range(MEMBERS):
            lane = (reach * MEMBERS + member) * TILE
            total = total + jnp.dot(
                counts_ref[:, lane : lane + TILE],
                block_of(ids_ref, pieces, reach, member),
                preferred_element_type=f32,
            )
    degree = degree_ref[...]
    pre = total / degree + bias_ref[...]
    sigma = jax.nn.sigmoid(pre)
    hidden = (pre * sigma).astype(bf16)
    hidden_ref[...] = jnp.where(first, hidden[:TILE], hidden[TILE:])
    hidden_other_ref[...] = jnp.where(first, hidden[TILE:], hidden[:TILE])
    up_mine = jnp.where(first, up_ref[:, :HALF], up_ref[:, HALF:])
    up_other = up_other_ref[...]
    up = jnp.concatenate(
        [jnp.where(first, up_mine, up_other), jnp.where(first, up_other, up_mine)], axis=0
    )
    grad_pre = up.astype(f32) * sigma * (1.0 + pre * (1.0 - sigma))
    scaled = (grad_pre / degree).astype(bf16).reshape(2, TILE, HALF)
    scaled_ref[...] = scaled
    for k in range(RUN):
        copies_ref[k] = scaled
    bias_out_ref[...] = jnp.sum(grad_pre, axis=0, keepdims=True)


def forward_math(ids, counts, total, degree, bias, upstream, up_other, pieces):
    return pl.pallas_call(
        forward_kernel,
        in_specs=[SMEM_SPEC] + [VMEM_SPEC] * (5 + PIECES),
        out_shape=(
            jax.ShapeDtypeStruct((TILE, HALF), bf16),
            jax.ShapeDtypeStruct((TILE, HALF), bf16),
            jax.ShapeDtypeStruct((RUN, 2, TILE, HALF), bf16),
            jax.ShapeDtypeStruct((2, TILE, HALF), bf16),
            jax.ShapeDtypeStruct((1, HALF), f32),
        ),
        name="forward_math",
    )(ids, counts, total, degree, bias, upstream, up_other, *pieces)


def backward_kernel(ids_ref, counts_ref, total_ref, bias_ref, feats_ref, feats_other_ref, *refs):
    pieces = (None,) + refs[: PIECES - 1]
    own_ref, other_ref, slab_ref, round_ref = refs[PIECES - 1 :]
    run, core = ids_ref[1], ids_ref[2]
    group = MEMBERS * TILE
    total = total_ref[...]
    for reach in (0, 2):
        rows = [block_of(ids_ref, pieces, reach, member) for member in range(MEMBERS)]
        total = total + jnp.dot(
            counts_ref[:, reach * group : reach * group + group],
            jnp.concatenate(rows, axis=0),
            preferred_element_type=f32,
        )
    round_ref[...] = total.astype(bf16).reshape(MEMBERS, TILE, HALF)
    own_ref[...] = round_ref[run * 2 + core]
    other_ref[...] = round_ref[run * 2 + 1 - core]
    part = jnp.zeros((F_RUN, HALF), f32)
    for feats, side in ((feats_ref, core), (feats_other_ref, 1 - core)):
        rows = jnp.concatenate([round_ref[k * 2 + side] for k in range(RUN)], axis=0)
        part = part + lax.dot_general(
            feats[...].reshape(RUN * TILE, F_RUN),
            rows,
            (((0,), (0,)), ((), ())),
            preferred_element_type=f32,
        )
    part = part.astype(bf16)
    for row in range(F_RUN // 16):
        for lane in range(2):
            slab_ref[row * 2 + lane] = part[row * 16 : row * 16 + 16, lane * 128 : lane * 128 + 128]
    slab_ref[BIAS_SLAB] = bias_ref[...]
    for rest in range(BIAS_SLAB + 1, SLABS):
        slab_ref[rest] = jnp.zeros((16, 128), bf16)


def backward_math(ids, counts, total, bias_rows, feats, feats_other, pieces):
    return pl.pallas_call(
        backward_kernel,
        in_specs=[SMEM_SPEC] + [VMEM_SPEC] * (4 + PIECES),
        out_shape=(
            jax.ShapeDtypeStruct((TILE, HALF), bf16),
            jax.ShapeDtypeStruct((TILE, HALF), bf16),
            jax.ShapeDtypeStruct((SLABS, 16, 128), bf16),
        ),
        scratch_shapes=[pltpu.VMEM((MEMBERS, TILE, HALF), bf16)],
        name="backward_math",
    )(ids, counts, total, bias_rows, feats, feats_other, *pieces)


def assemble_kernel(ids_ref, mine_ref, other_ref, weight_ref, bias_ref):
    first = ids_ref[2] == 0
    bias = [jnp.zeros((2, 128), f32), jnp.zeros((2, 128), f32)]
    for x in range(4):
        for column in range(64):
            yh, run, z = column // 32, (column // 8) % 4, column % 8
            slab = (yh * 4 + x) * 8 + z
            if slab > BIAS_SLAB:
                continue
            mine, other = mine_ref[x, column], other_ref[x, column]
            for core in range(2):
                keep = first if core == 0 else jnp.logical_not(first)
                value = jnp.where(keep, mine, other)
                if slab == BIAS_SLAB:
                    rows = value.astype(f32)
                    bias[core] = bias[core] + (rows[:2] + rows[2:4])
                else:
                    row, lane = run * F_RUN + (slab // 2) * 16, core * HALF + (slab % 2) * 128
                    weight_ref[row : row + 16, lane : lane + 128] = value
    bias_ref[:2, :] = bias[0]
    bias_ref[2:, :] = bias[1]


def assemble(ids, mine, other):
    return pl.pallas_call(
        assemble_kernel,
        in_specs=[SMEM_SPEC] + [VMEM_SPEC] * 2,
        out_shape=(
            jax.ShapeDtypeStruct((RUN * F_RUN, HID), bf16),
            jax.ShapeDtypeStruct((4, 128), f32),
        ),
        name="assemble",
    )(ids, mine, other)


def high_low(value):
    high = lax.reduce_precision(value, 8, 7)
    return jnp.concatenate([high, value - high, jnp.zeros((12, 128), f32)], axis=0).astype(bf16)


def on_device(features, weight, bias, tile_cols, tile_count, nbr_slot, nbr_col, nbr_keep, upstream):
    group = (lax.axis_index("yh") * 4 + lax.axis_index("x")) * 8 + lax.axis_index("z")
    core = lax.axis_index("c")
    first = core == 0
    far_low, far_high = group % 32 == 0, group % 32 == 31
    ids = jnp.stack([group, lax.axis_index("yl"), core, far_low, far_high]).astype(i32)

    copies, same, cross = project(
        ids, tile_count, tile_cols, nbr_slot.T, nbr_col.T, nbr_keep.T, features, weight
    )
    straight, turned = across(same, cross)
    own = lax.all_to_all(copies, ("yl", "c"), 0, 0)
    tied, _ = lax.optimization_barrier((upstream, copies))
    up_other = swap_core(jnp.where(first, tied[:, HALF:], tied[:, :HALF]))
    slices = jnp.stack([features[:, k * F_RUN : (k + 1) * F_RUN] for k in range(RUN)])
    own, up_other, slices = lax.optimization_barrier((own, up_other, slices))
    straight, turned, _ = lax.optimization_barrier((straight, turned, own))
    received = jnp.stack([jnp.where(first, straight, turned), jnp.where(first, turned, straight)])
    low, high = neighbours(own)
    parts = along_run(received)
    counts, degree = forward_counts(ids, own)
    feats = lax.all_to_all(slices, "yl", 0, 0)
    feats_other = swap_core(feats)
    pieces = (own, low, high) + parts
    bias_half = jnp.where(first, bias[:HALF], bias[HALF:])[None]
    hidden_mine, hidden_send, scaled_copies, scaled, bias_part = forward_math(
        ids, counts, forward_own(ids, counts, own), degree, bias_half, upstream, up_other,
        pieces[1:],
    )

    received = across(scaled, None)
    own = lax.all_to_all(scaled_copies, "yl", 0, 0)
    hidden_got = swap_core(hidden_send)
    counts_back = backward_counts(ids, pieces)
    received, own, counts_back = lax.optimization_barrier((received, own, counts_back))
    own = own.reshape(MEMBERS, TILE, HALF)
    low, high = neighbours(own)
    parts = along_run(received)
    round_mine, round_send, slabs = backward_math(
        ids, counts_back, backward_own(counts_back, own), high_low(bias_part.reshape(2, 128)),
        feats, feats_other, (low, high) + parts,
    )
    round_got = swap_core(round_send)
    own_round = jnp.where(
        first,
        jnp.concatenate([round_mine, round_got], axis=1),
        jnp.concatenate([round_got, round_mine], axis=1),
    )
    grad_features = lax.dot_general(
        own_round, weight, (((1,), (1,)), ((), ())), preferred_element_type=f32
    ).astype(bf16)
    hidden = jnp.where(
        first,
        jnp.concatenate([hidden_mine, hidden_got], axis=1),
        jnp.concatenate([hidden_got, hidden_mine], axis=1),
    )
    terms = lax.all_to_all(slabs, WIDE, 0, 0)
    terms, grad_features, hidden = lax.optimization_barrier((terms, grad_features, hidden))
    reduced = jnp.sum(terms.astype(f32), axis=0)
    piece = jnp.where(
        group == BIAS_SLAB, high_low(reduced[:2] + reduced[2:4]), reduced.astype(bf16)
    )
    column = spread_to(piece, ("yh", "yl", "z"), 64)
    plane = spread_to(column, "x", 4)
    weight_grad, bias_grad = assemble(ids, plane, swap_core(plane))
    return hidden, grad_features, weight_grad, bias_grad.reshape(HID)


def solution(mesh):
    split = Mesh(mesh.devices.reshape(SIZES), AXES)
    rows = P(AXES, None)
    in_specs = (rows, P(), P(), rows, P(AXES), rows, rows, rows, rows)
    out_specs = (rows, rows, P(), P())
    return jax.shard_map(
        on_device, mesh=split, in_specs=in_specs, out_specs=out_specs, check_vma=False
    )
```

```python
import jax
import jax.numpy as jnp
from jax import lax
from jax.experimental import pallas as pl
from jax.experimental.pallas import tpu as pltpu
from jax.sharding import Mesh
from jax.sharding import PartitionSpec as P

TILE = 128
KNN = 15
KEYS = 16
HID = 512
HALF = 256
AXES = ("yh", "x", "z", "yl", "c")
SIZES = (2, 4, 8, 4, 2)
WIDE = ("yh", "x", "z")
GROUPS = 64
RUN = 4
MEMBERS = 8
REACH = 3
PIECES = 7
WINDOW = REACH * MEMBERS * TILE
BLOCKS = 512
DEAD = 31
F_RUN = 448
SLABS = 64
BIAS_SLAB = 56

i32 = jnp.int32
bf16 = jnp.bfloat16
f32 = jnp.float32

EAGER = pl.CostEstimate(flops=4_000_000_000, transcendentals=0, bytes_accessed=8_000_000)
SMEM_SPEC = pl.BlockSpec(memory_space=pltpu.SMEM)
VMEM_SPEC = pl.BlockSpec(memory_space=pltpu.VMEM)


def spread_to(shard, axes, count):
    return lax.all_to_all(jnp.broadcast_to(shard[None], (count,) + shard.shape), axes, 0, 0)


FAR = ((31, 32), (63, 0), (32, 31), (0, 63))


def device(group, run, core):
    return (group * RUN + run) * 2 + core


def across(same, cross):
    pairs = [(a, b, r, c) for a, b in FAR for r in range(RUN) for c in range(2)]
    straight = [(device(a, r, c), device(b, r, c)) for a, b, r, c in pairs]
    turned = [(device(a, r, c), device(b, r, 1 - c)) for a, b, r, c in pairs]
    got = lax.ppermute(same, AXES, straight)
    return got if cross is None else (got, lax.ppermute(cross, AXES, turned))


def along_run(block):
    parts = [block]
    for step in range(1, RUN):
        pairs = [
            (device(a, r, c), device(a, r ^ step, c))
            for a, _ in FAR for r in range(RUN) for c in range(2)
        ]
        parts.append(lax.ppermute(block, AXES, pairs))
    return tuple(parts)


def block_of(ids_ref, pieces, reach, member):
    own, low, high = pieces[:REACH]
    if reach == 1:
        return own[member, :TILE, :]
    near = (low, high)[reach // 2][member, :TILE, :]
    far = pieces[REACH + member // 2][member % 2, :TILE, :]
    return jnp.where(ids_ref[3 + reach // 2] > 0, far, near)


def keys_of(ids_ref, pieces, reach, member):
    own, low, high = pieces[:REACH]
    if reach == 1:
        return own[member, TILE:, :].astype(f32)
    near = (low, high)[reach // 2][member, TILE:, :].astype(f32)
    far = pieces[REACH + member // 2][member % 2, TILE:, :].astype(f32)
    return jnp.where(ids_ref[3 + reach // 2] > 0, far, near)


def neighbours(block):
    forward = [(i, (i + 1) % GROUPS) for i in range(GROUPS) if i % 32 != 31]
    backward = [(target, source) for source, target in forward]
    return lax.ppermute(block, WIDE, forward), lax.ppermute(block, WIDE, backward)


def swap_core(block):
    return lax.ppermute(block, "c", [(0, 1), (1, 0)])


def project_kernel(ids_ref, count_ref, tiles_ref, slot_ref, col_ref, keep_ref, features_ref, weight_ref,
                   copies_ref, same_ref, cross_ref):
    base = (ids_ref[0] - 1) * MEMBERS
    slot = slot_ref[...]
    live = keep_ref[...] * (slot < count_ref[0]).astype(i32)
    position = jnp.zeros_like(slot)
    for k in range(tiles_ref.shape[1]):
        block = tiles_ref[0, k] - base
        block = jnp.where(block < 0, block + BLOCKS, block)
        block = jnp.where(block >= BLOCKS, block - BLOCKS, block)
        position = position + jnp.where(slot == k, block, 0)
    pad = jnp.zeros((KEYS - KNN, TILE), i32)

    def rows(value):
        return jnp.concatenate([value, pad], axis=0)

    dead = rows(1 - live) + lax.broadcasted_iota(i32, (KEYS, TILE), 0) // KNN
    blocks = jnp.where(dead > 0, DEAD, rows(position))
    keys = jnp.concatenate([blocks, rows(col_ref[...])], axis=1).astype(f32).astype(bf16)
    projected = jnp.dot(features_ref[...], weight_ref[...], preferred_element_type=f32).astype(bf16)
    for k in range(MEMBERS):
        half = (k % 2) * HALF
        copies_ref[k, :TILE, :] = projected[:, half : half + HALF]
        copies_ref[k, TILE:, :] = keys
    first = ids_ref[2] == 0
    left, right = projected[:, :HALF], projected[:, HALF:]
    same_ref[:TILE, :] = jnp.where(first, left, right)
    same_ref[TILE:, :] = keys
    cross_ref[:TILE, :] = jnp.where(first, right, left)
    cross_ref[TILE:, :] = keys


def project(ids, tile_count, tile_cols, slot, col, keep, features, weight):
    return pl.pallas_call(
        project_kernel,
        in_specs=[SMEM_SPEC] * 3 + [VMEM_SPEC] * 5,
        out_shape=(
            jax.ShapeDtypeStruct((MEMBERS, TILE + KEYS, HALF), bf16),
            jax.ShapeDtypeStruct((TILE + KEYS, HALF), bf16),
            jax.ShapeDtypeStruct((TILE + KEYS, HALF), bf16),
        ),
        name="project",
    )(ids, tile_count, tile_cols, slot, col, keep, features, weight)


def digits_of(block, wanted):
    valid = lax.shift_right_arithmetic(block, 3) == wanted
    shift = 4 * jnp.bitwise_and(block, 7)
    return jnp.where(valid, lax.shift_left(jnp.ones_like(shift), shift), 0)


def forward_counts_kernel(ids_ref, own_ref, counts_ref, degree_ref):
    run = ids_ref[1]
    for core in range(2):
        keys = own_ref[run * 2 + core, TILE:, :].astype(f32).astype(i32).T
        block, cells = keys[:TILE, :], keys[TILE:, :]
        live = jnp.where(block < DEAD, 1.0, 0.0)
        degree_ref[core * TILE : core * TILE + TILE, :] = 1.0 + jnp.sum(live, axis=1, keepdims=True)
        reach_of = lax.shift_right_logical(block, 3)
        low_twist = jnp.where(reach_of == 0, ids_ref[3] * run * 2, 0)
        twist = low_twist + jnp.where(reach_of == 2, ids_ref[4] * run * 2, 0)
        block = jnp.bitwise_xor(block, twist)
        digits = [digits_of(block, reach) for reach in range(REACH)]
        lanes = lax.broadcasted_iota(i32, (16, 128), 1)
        for step in range(TILE // 16):
            here = slice(step * 16, step * 16 + 16)
            totals = [jnp.zeros((16, 128), i32) for _ in range(REACH)]
            for e in range(KNN):
                hit = cells[here, e : e + 1] == lanes
                for reach in range(REACH):
                    totals[reach] = totals[reach] + jnp.where(hit, digits[reach][here, e : e + 1], 0)
            row = core * TILE + step * 16
            for tile in range(REACH * MEMBERS):
                digit = lax.shift_right_logical(totals[tile // 8], 4 * (tile % 8))
                count = jnp.bitwise_and(digit, 15).astype(f32).astype(bf16)
                counts_ref[row : row + 16, tile * 128 : tile * 128 + 128] = count


def forward_counts(ids, own):
    return pl.pallas_call(
        forward_counts_kernel,
        in_specs=[SMEM_SPEC, VMEM_SPEC],
        out_shape=(
            jax.ShapeDtypeStruct((2 * TILE, WINDOW), bf16),
            jax.ShapeDtypeStruct((2 * TILE, 1), f32),
        ),
        cost_estimate=EAGER,
        name="forward_counts",
    )(ids, own)


def backward_counts_kernel(ids_ref, *refs):
    pieces, out_ref = refs[:PIECES], refs[PIECES]
    for member in range(MEMBERS):
        for reach in range(REACH):
            keys = keys_of(ids_ref, pieces, reach, member).astype(i32)
            digits = digits_of(keys[:, :TILE], REACH - 1 - reach)
            cells = keys[:, TILE:]
            lane = (reach * MEMBERS + member) * TILE
            for step in range(TILE // 16):
                rows = lax.broadcasted_iota(i32, (16, 128), 0) + step * 16
                total = jnp.zeros((16, 128), i32)
                for e in range(KNN):
                    total = total + jnp.where(cells[e : e + 1, :] == rows, digits[e : e + 1, :], 0)
                for k in range(MEMBERS):
                    count = jnp.bitwise_and(lax.shift_right_logical(total, 4 * k), 15)
                    at = k * TILE + step * 16
                    out_ref[at : at + 16, lane : lane + TILE] = count.astype(f32).astype(bf16)


def backward_counts(ids, pieces):
    return pl.pallas_call(
        backward_counts_kernel,
        in_specs=[SMEM_SPEC] + [VMEM_SPEC] * PIECES,
        out_shape=jax.ShapeDtypeStruct((MEMBERS * TILE, WINDOW), bf16),
        cost_estimate=EAGER,
        name="backward_counts",
    )(ids, *pieces)


def forward_own_kernel(ids_ref, counts_ref, own_ref, total_ref):
    run = ids_ref[1]
    total = jnp.concatenate(
        [own_ref[run * 2 + core, :TILE, :].astype(f32) for core in range(2)], axis=0
    )
    for member in range(MEMBERS):
        lane = (MEMBERS + member) * TILE
        total = total + jnp.dot(
            counts_ref[:, lane : lane + TILE],
            own_ref[member, :TILE, :],
            preferred_element_type=f32,
        )
    total_ref[...] = total


def forward_own(ids, counts, own):
    return pl.pallas_call(
        forward_own_kernel,
        in_specs=[SMEM_SPEC] + [VMEM_SPEC] * 2,
        out_shape=jax.ShapeDtypeStruct((2 * TILE, HALF), f32),
        cost_estimate=EAGER,
        name="forward_own",
    )(ids, counts, own)


def backward_own_kernel(counts_ref, own_ref, total_ref):
    group = MEMBERS * TILE
    own = own_ref[...].reshape(group, HALF)
    total_ref[...] = own.astype(f32) + jnp.dot(
        counts_ref[:, group : 2 * group], own, preferred_element_type=f32
    )


def backward_own(counts, own):
    return pl.pallas_call(
        backward_own_kernel,
        in_specs=[VMEM_SPEC] * 2,
        out_shape=jax.ShapeDtypeStruct((MEMBERS * TILE, HALF), f32),
        cost_estimate=EAGER,
        name="backward_own",
    )(counts, own)


def forward_kernel(
    ids_ref, counts_ref, total_ref, degree_ref, bias_ref, up_ref, up_other_ref, *refs
):
    pieces = (None,) + refs[: PIECES - 1]
    hidden_ref, hidden_other_ref, copies_ref, scaled_ref, bias_out_ref = refs[PIECES - 1 :]
    first = ids_ref[2] == 0
    total = total_ref[...]
    for reach in (0, 2):
        for member in range(MEMBERS):
            lane = (reach * MEMBERS + member) * TILE
            total = total + jnp.dot(
                counts_ref[:, lane : lane + TILE],
                block_of(ids_ref, pieces, reach, member),
                preferred_element_type=f32,
            )
    degree = degree_ref[...]
    pre = total / degree + bias_ref[...]
    sigma = jax.nn.sigmoid(pre)
    hidden = (pre * sigma).astype(bf16)
    hidden_ref[...] = jnp.where(first, hidden[:TILE], hidden[TILE:])
    hidden_other_ref[...] = jnp.where(first, hidden[TILE:], hidden[:TILE])
    up_mine = jnp.where(first, up_ref[:, :HALF], up_ref[:, HALF:])
    up_other = up_other_ref[...]
    up = jnp.concatenate(
        [jnp.where(first, up_mine, up_other), jnp.where(first, up_other, up_mine)], axis=0
    )
    grad_pre = up.astype(f32) * sigma * (1.0 + pre * (1.0 - sigma))
    scaled = (grad_pre / degree).astype(bf16).reshape(2, TILE, HALF)
    scaled_ref[...] = scaled
    for k in range(RUN):
        copies_ref[k] = scaled
    bias_out_ref[...] = jnp.sum(grad_pre, axis=0, keepdims=True)


def forward_math(ids, counts, total, degree, bias, upstream, up_other, pieces):
    return pl.pallas_call(
        forward_kernel,
        in_specs=[SMEM_SPEC] + [VMEM_SPEC] * (5 + PIECES),
        out_shape=(
            jax.ShapeDtypeStruct((TILE, HALF), bf16),
            jax.ShapeDtypeStruct((TILE, HALF), bf16),
            jax.ShapeDtypeStruct((RUN, 2, TILE, HALF), bf16),
            jax.ShapeDtypeStruct((2, TILE, HALF), bf16),
            jax.ShapeDtypeStruct((1, HALF), f32),
        ),
        name="forward_math",
    )(ids, counts, total, degree, bias, upstream, up_other, *pieces)


def backward_kernel(ids_ref, counts_ref, total_ref, bias_ref, feats_ref, feats_other_ref, *refs):
    pieces = (None,) + refs[: PIECES - 1]
    own_ref, other_ref, slab_ref, round_ref = refs[PIECES - 1 :]
    run, core = ids_ref[1], ids_ref[2]
    group = MEMBERS * TILE
    total = total_ref[...]
    for reach in (0, 2):
        rows = [block_of(ids_ref, pieces, reach, member) for member in range(MEMBERS)]
        total = total + jnp.dot(
            counts_ref[:, reach * group : reach * group + group],
            jnp.concatenate(rows, axis=0),
            preferred_element_type=f32,
        )
    round_ref[...] = total.astype(bf16).reshape(MEMBERS, TILE, HALF)
    own_ref[...] = round_ref[run * 2 + core]
    other_ref[...] = round_ref[run * 2 + 1 - core]
    part = jnp.zeros((F_RUN, HALF), f32)
    for feats, side in ((feats_ref, core), (feats_other_ref, 1 - core)):
        rows = jnp.concatenate([round_ref[k * 2 + side] for k in range(RUN)], axis=0)
        part = part + lax.dot_general(
            feats[...].reshape(RUN * TILE, F_RUN),
            rows,
            (((0,), (0,)), ((), ())),
            preferred_element_type=f32,
        )
    part = part.astype(bf16)
    for row in range(F_RUN // 16):
        for lane in range(2):
            slab_ref[row * 2 + lane] = part[row * 16 : row * 16 + 16, lane * 128 : lane * 128 + 128]
    slab_ref[BIAS_SLAB] = bias_ref[...]
    for rest in range(BIAS_SLAB + 1, SLABS):
        slab_ref[rest] = jnp.zeros((16, 128), bf16)


def backward_math(ids, counts, total, bias_rows, feats, feats_other, pieces):
    return pl.pallas_call(
        backward_kernel,
        in_specs=[SMEM_SPEC] + [VMEM_SPEC] * (4 + PIECES),
        out_shape=(
            jax.ShapeDtypeStruct((TILE, HALF), bf16),
            jax.ShapeDtypeStruct((TILE, HALF), bf16),
            jax.ShapeDtypeStruct((SLABS, 16, 128), bf16),
        ),
        scratch_shapes=[pltpu.VMEM((MEMBERS, TILE, HALF), bf16)],
        name="backward_math",
    )(ids, counts, total, bias_rows, feats, feats_other, *pieces)


def assemble_kernel(ids_ref, *refs):
    mine, other, (weight_ref, bias_ref) = refs[:4], refs[4:8], refs[8:]
    first = ids_ref[2] == 0
    for k in range(4):
        x = jnp.bitwise_xor(ids_ref[5], k)
        for yh in range(2):

            def place(k=k, yh=yh):
                for run in range(RUN):
                    for z in range(8):
                        column = (yh * RUN + run) * 8 + z
                        row = run * F_RUN + yh * 256 + (z // 2) * 16
                        here = pl.ds(pl.multiple_of(row + x * 64, 16), 16)
                        for core in range(2):
                            keep = first if core == 0 else jnp.logical_not(first)
                            value = jnp.where(keep, mine[k][column], other[k][column])
                            lane = core * HALF + (z % 2) * 128
                            weight_ref[here, lane : lane + 128] = value

            def total(k=k, yh=yh):
                for core in range(2):
                    keep = first if core == 0 else jnp.logical_not(first)
                    bias = jnp.zeros((2, 128), f32)
                    for run in range(RUN):
                        column = (yh * RUN + run) * 8
                        rows = jnp.where(keep, mine[k][column], other[k][column]).astype(f32)
                        bias = bias + (rows[:2] + rows[2:4])
                    bias_ref[core * 2 : core * 2 + 2, :] = bias

            if yh == 0:
                place()
            else:
                pl.when(x != 3)(place)
                pl.when(x == 3)(total)


def assemble(ids, mine, other):
    return pl.pallas_call(
        assemble_kernel,
        in_specs=[SMEM_SPEC] + [VMEM_SPEC] * 8,
        out_shape=(
            jax.ShapeDtypeStruct((RUN * F_RUN, HID), bf16),
            jax.ShapeDtypeStruct((4, 128), f32),
        ),
        name="assemble",
    )(ids, *mine, *other)


def high_low(value):
    high = lax.reduce_precision(value, 8, 7)
    return jnp.concatenate([high, value - high, jnp.zeros((12, 128), f32)], axis=0).astype(bf16)


def on_device(features, weight, bias, tile_cols, tile_count, nbr_slot, nbr_col, nbr_keep, upstream):
    group = (lax.axis_index("yh") * 4 + lax.axis_index("x")) * 8 + lax.axis_index("z")
    core = lax.axis_index("c")
    first = core == 0
    far_low, far_high = group % 32 == 0, group % 32 == 31
    ids = jnp.stack([group, lax.axis_index("yl"), core, far_low, far_high, lax.axis_index("x")]).astype(i32)

    copies, same, cross = project(
        ids, tile_count, tile_cols, nbr_slot.T, nbr_col.T, nbr_keep.T, features, weight
    )
    straight, turned = across(same, cross)
    own = lax.all_to_all(copies, ("yl", "c"), 0, 0)
    slices = jnp.stack([features[:, k * F_RUN : (k + 1) * F_RUN] for k in range(RUN)])
    tied, _ = lax.optimization_barrier((upstream, copies))
    up_other = swap_core(jnp.where(first, tied[:, HALF:], tied[:, :HALF]))
    own, up_other, slices = lax.optimization_barrier((own, up_other, slices))
    low, high = neighbours(own)
    counts, degree = forward_counts(ids, own)
    own_total = forward_own(ids, counts, own)
    straight, turned, own_total = lax.optimization_barrier((straight, turned, own_total))
    received = jnp.stack([jnp.where(first, straight, turned), jnp.where(first, turned, straight)])
    parts = along_run(received)
    feats = lax.all_to_all(slices, "yl", 0, 0)
    feats_other = swap_core(feats)
    pieces = (own, low, high) + parts
    bias_half = jnp.where(first, bias[:HALF], bias[HALF:])[None]
    hidden_mine, hidden_send, scaled_copies, scaled, bias_part = forward_math(
        ids, counts, own_total, degree, bias_half, upstream, up_other, pieces[1:]
    )

    received = across(scaled, None)
    own = lax.all_to_all(scaled_copies, "yl", 0, 0)
    hidden_got = swap_core(hidden_send)
    counts_back = backward_counts(ids, pieces)
    received, own, counts_back = lax.optimization_barrier((received, own, counts_back))
    own = own.reshape(MEMBERS, TILE, HALF)
    low, high = neighbours(own)
    parts = along_run(received)
    round_mine, round_send, slabs = backward_math(
        ids, counts_back, backward_own(counts_back, own), high_low(bias_part.reshape(2, 128)),
        feats, feats_other, (low, high) + parts,
    )
    round_got = swap_core(round_send)
    own_round = jnp.where(
        first,
        jnp.concatenate([round_mine, round_got], axis=1),
        jnp.concatenate([round_got, round_mine], axis=1),
    )
    grad_features = lax.dot_general(
        own_round, weight, (((1,), (1,)), ((), ())), preferred_element_type=f32
    ).astype(bf16)
    hidden = jnp.where(
        first,
        jnp.concatenate([hidden_mine, hidden_got], axis=1),
        jnp.concatenate([hidden_got, hidden_mine], axis=1),
    )
    terms = lax.all_to_all(slabs, WIDE, 0, 0)
    terms, grad_features, hidden = lax.optimization_barrier((terms, grad_features, hidden))
    reduced = jnp.sum(terms.astype(f32), axis=0)
    piece = jnp.where(
        group == BIAS_SLAB, high_low(reduced[:2] + reduced[2:4]), reduced.astype(bf16)
    )
    column = spread_to(piece, ("yh", "yl", "z"), 64)
    columns = [column]
    for step in (2, 1, 3):
        columns.append(lax.ppermute(column, "x", [(i, i ^ step) for i in range(4)]))
    columns = [columns[0], columns[2], columns[1], columns[3]]
    weight_grad, bias_grad = assemble(ids, columns, [swap_core(block) for block in columns])
    return hidden, grad_features, weight_grad, bias_grad.reshape(HID)


def solution(mesh):
    split = Mesh(mesh.devices.reshape(SIZES), AXES)
    rows = P(AXES, None)
    in_specs = (rows, P(), P(), rows, P(AXES), rows, rows, rows, rows)
    out_specs = (rows, rows, P(), P())
    return jax.shard_map(
        on_device, mesh=split, in_specs=in_specs, out_specs=out_specs, check_vma=False
    )
```

```python
import jax
import jax.numpy as jnp
from jax import lax
from jax.experimental import pallas as pl
from jax.experimental.pallas import tpu as pltpu
from jax.sharding import Mesh
from jax.sharding import PartitionSpec as P

TILE = 128
KNN = 15
KEYS = 16
HID = 512
HALF = 256
AXES = ("yh", "x", "z", "yl", "c")
SIZES = (2, 4, 8, 4, 2)
WIDE = ("yh", "x", "z")
GROUPS = 64
RUN = 4
MEMBERS = 8
REACH = 3
PIECES = 7
WINDOW = REACH * MEMBERS * TILE
BLOCKS = 512
DEAD = 31
F_RUN = 448
SLABS = 64
BIAS_SLAB = 56

i32 = jnp.int32
bf16 = jnp.bfloat16
f32 = jnp.float32

EAGER = pl.CostEstimate(flops=4_000_000_000, transcendentals=0, bytes_accessed=8_000_000)
SMEM_SPEC = pl.BlockSpec(memory_space=pltpu.SMEM)
VMEM_SPEC = pl.BlockSpec(memory_space=pltpu.VMEM)


def spread_to(shard, axes, count):
    return lax.all_to_all(jnp.broadcast_to(shard[None], (count,) + shard.shape), axes, 0, 0)


FAR = ((31, 32), (63, 0), (32, 31), (0, 63))


def device(group, run, core):
    return (group * RUN + run) * 2 + core


def across(same, cross):
    pairs = [(a, b, r, c) for a, b in FAR for r in range(RUN) for c in range(2)]
    straight = [(device(a, r, c), device(b, r, c)) for a, b, r, c in pairs]
    turned = [(device(a, r, c), device(b, r, 1 - c)) for a, b, r, c in pairs]
    got = lax.ppermute(same, AXES, straight)
    return got if cross is None else (got, lax.ppermute(cross, AXES, turned))


def along_run(block):
    parts = [block]
    for step in range(1, RUN):
        pairs = [
            (device(a, r, c), device(a, r ^ step, c))
            for a, _ in FAR for r in range(RUN) for c in range(2)
        ]
        parts.append(lax.ppermute(block, AXES, pairs))
    return tuple(parts)


def block_of(ids_ref, pieces, reach, member):
    own, low, high = pieces[:REACH]
    if reach == 1:
        return own[member, :TILE, :]
    near = (low, high)[reach // 2][member, :TILE, :]
    far = pieces[REACH + member // 2][member % 2, :TILE, :]
    return jnp.where(ids_ref[3 + reach // 2] > 0, far, near)


def keys_of(ids_ref, pieces, reach, member):
    own, low, high = pieces[:REACH]
    if reach == 1:
        return own[member, TILE:, :].astype(f32)
    near = (low, high)[reach // 2][member, TILE:, :].astype(f32)
    far = pieces[REACH + member // 2][member % 2, TILE:, :].astype(f32)
    return jnp.where(ids_ref[3 + reach // 2] > 0, far, near)


def neighbours(block):
    forward = [(i, (i + 1) % GROUPS) for i in range(GROUPS) if i % 32 != 31]
    backward = [(target, source) for source, target in forward]
    return lax.ppermute(block, WIDE, forward), lax.ppermute(block, WIDE, backward)


def swap_core(block):
    return lax.ppermute(block, "c", [(0, 1), (1, 0)])


def project_kernel(ids_ref, count_ref, tiles_ref, slot_ref, col_ref, keep_ref, features_ref, weight_ref,
                   copies_ref, same_ref, cross_ref):
    base = (ids_ref[0] - 1) * MEMBERS
    slot = slot_ref[...]
    live = keep_ref[...] * (slot < count_ref[0]).astype(i32)
    position = jnp.zeros_like(slot)
    for k in range(tiles_ref.shape[1]):
        block = tiles_ref[0, k] - base
        block = jnp.where(block < 0, block + BLOCKS, block)
        block = jnp.where(block >= BLOCKS, block - BLOCKS, block)
        position = position + jnp.where(slot == k, block, 0)
    pad = jnp.zeros((KEYS - KNN, TILE), i32)

    def rows(value):
        return jnp.concatenate([value, pad], axis=0)

    dead = rows(1 - live) + lax.broadcasted_iota(i32, (KEYS, TILE), 0) // KNN
    blocks = jnp.where(dead > 0, DEAD, rows(position))
    keys = jnp.concatenate([blocks, rows(col_ref[...])], axis=1).astype(f32).astype(bf16)
    projected = jnp.dot(features_ref[...], weight_ref[...], preferred_element_type=f32).astype(bf16)
    for k in range(MEMBERS):
        half = (k % 2) * HALF
        copies_ref[k, :TILE, :] = projected[:, half : half + HALF]
        copies_ref[k, TILE:, :] = keys
    first = ids_ref[2] == 0
    left, right = projected[:, :HALF], projected[:, HALF:]
    same_ref[:TILE, :] = jnp.where(first, left, right)
    same_ref[TILE:, :] = keys
    cross_ref[:TILE, :] = jnp.where(first, right, left)
    cross_ref[TILE:, :] = keys


def project(ids, tile_count, tile_cols, slot, col, keep, features, weight):
    return pl.pallas_call(
        project_kernel,
        in_specs=[SMEM_SPEC] * 3 + [VMEM_SPEC] * 5,
        out_shape=(
            jax.ShapeDtypeStruct((MEMBERS, TILE + KEYS, HALF), bf16),
            jax.ShapeDtypeStruct((TILE + KEYS, HALF), bf16),
            jax.ShapeDtypeStruct((TILE + KEYS, HALF), bf16),
        ),
        name="project",
    )(ids, tile_count, tile_cols, slot, col, keep, features, weight)


def digits_of(block, wanted):
    valid = lax.shift_right_arithmetic(block, 3) == wanted
    shift = 4 * jnp.bitwise_and(block, 7)
    return jnp.where(valid, lax.shift_left(jnp.ones_like(shift), shift), 0)


def forward_counts_kernel(ids_ref, own_ref, counts_ref, degree_ref):
    run = ids_ref[1]
    for core in range(2):
        keys = own_ref[run * 2 + core, TILE:, :].astype(f32).astype(i32).T
        block, cells = keys[:TILE, :], keys[TILE:, :]
        live = jnp.where(block < DEAD, 1.0, 0.0)
        degree_ref[core * TILE : core * TILE + TILE, :] = 1.0 + jnp.sum(live, axis=1, keepdims=True)
        reach_of = lax.shift_right_logical(block, 3)
        low_twist = jnp.where(reach_of == 0, ids_ref[3] * run * 2, 0)
        twist = low_twist + jnp.where(reach_of == 2, ids_ref[4] * run * 2, 0)
        block = jnp.bitwise_xor(block, twist)
        digits = [digits_of(block, reach) for reach in range(REACH)]
        lanes = lax.broadcasted_iota(i32, (16, 128), 1)
        for step in range(TILE // 16):
            here = slice(step * 16, step * 16 + 16)
            totals = [jnp.zeros((16, 128), i32) for _ in range(REACH)]
            for e in range(KNN):
                hit = cells[here, e : e + 1] == lanes
                for reach in range(REACH):
                    totals[reach] = totals[reach] + jnp.where(hit, digits[reach][here, e : e + 1], 0)
            row = core * TILE + step * 16
            for tile in range(REACH * MEMBERS):
                digit = lax.shift_right_logical(totals[tile // 8], 4 * (tile % 8))
                count = jnp.bitwise_and(digit, 15).astype(f32).astype(bf16)
                counts_ref[row : row + 16, tile * 128 : tile * 128 + 128] = count


def forward_counts(ids, own):
    return pl.pallas_call(
        forward_counts_kernel,
        in_specs=[SMEM_SPEC, VMEM_SPEC],
        out_shape=(
            jax.ShapeDtypeStruct((2 * TILE, WINDOW), bf16),
            jax.ShapeDtypeStruct((2 * TILE, 1), f32),
        ),
        cost_estimate=EAGER,
        name="forward_counts",
    )(ids, own)


def backward_counts_kernel(ids_ref, *refs):
    pieces, out_ref = refs[:PIECES], refs[PIECES]
    for member in range(MEMBERS):
        for reach in range(REACH):
            keys = keys_of(ids_ref, pieces, reach, member).astype(i32)
            digits = digits_of(keys[:, :TILE], REACH - 1 - reach)
            cells = keys[:, TILE:]
            lane = (reach * MEMBERS + member) * TILE
            for step in range(TILE // 16):
                rows = lax.broadcasted_iota(i32, (16, 128), 0) + step * 16
                total = jnp.zeros((16, 128), i32)
                for e in range(KNN):
                    total = total + jnp.where(cells[e : e + 1, :] == rows, digits[e : e + 1, :], 0)
                for k in range(MEMBERS):
                    count = jnp.bitwise_and(lax.shift_right_logical(total, 4 * k), 15)
                    at = k * TILE + step * 16
                    out_ref[at : at + 16, lane : lane + TILE] = count.astype(f32).astype(bf16)


def backward_counts(ids, pieces):
    return pl.pallas_call(
        backward_counts_kernel,
        in_specs=[SMEM_SPEC] + [VMEM_SPEC] * PIECES,
        out_shape=jax.ShapeDtypeStruct((MEMBERS * TILE, WINDOW), bf16),
        cost_estimate=EAGER,
        name="backward_counts",
    )(ids, *pieces)


def forward_own_kernel(ids_ref, counts_ref, own_ref, total_ref):
    run = ids_ref[1]
    total = jnp.concatenate(
        [own_ref[run * 2 + core, :TILE, :].astype(f32) for core in range(2)], axis=0
    )
    for member in range(MEMBERS):
        lane = (MEMBERS + member) * TILE
        total = total + jnp.dot(
            counts_ref[:, lane : lane + TILE],
            own_ref[member, :TILE, :],
            preferred_element_type=f32,
        )
    total_ref[...] = total


def forward_own(ids, counts, own):
    return pl.pallas_call(
        forward_own_kernel,
        in_specs=[SMEM_SPEC] + [VMEM_SPEC] * 2,
        out_shape=jax.ShapeDtypeStruct((2 * TILE, HALF), f32),
        cost_estimate=EAGER,
        name="forward_own",
    )(ids, counts, own)


def backward_own_kernel(counts_ref, own_ref, total_ref):
    group = MEMBERS * TILE
    own = own_ref[...].reshape(group, HALF)
    total_ref[...] = own.astype(f32) + jnp.dot(
        counts_ref[:, group : 2 * group], own, preferred_element_type=f32
    )


def backward_own(counts, own):
    return pl.pallas_call(
        backward_own_kernel,
        in_specs=[VMEM_SPEC] * 2,
        out_shape=jax.ShapeDtypeStruct((MEMBERS * TILE, HALF), f32),
        cost_estimate=EAGER,
        name="backward_own",
    )(counts, own)


def forward_kernel(
    ids_ref, counts_ref, total_ref, degree_ref, bias_ref, up_ref, up_other_ref, *refs
):
    pieces = (None,) + refs[: PIECES - 1]
    hidden_ref, hidden_other_ref, copies_ref, scaled_ref, bias_out_ref = refs[PIECES - 1 :]
    first = ids_ref[2] == 0
    total = total_ref[...]
    for reach in (0, 2):
        for member in range(MEMBERS):
            lane = (reach * MEMBERS + member) * TILE
            total = total + jnp.dot(
                counts_ref[:, lane : lane + TILE],
                block_of(ids_ref, pieces, reach, member),
                preferred_element_type=f32,
            )
    degree = degree_ref[...]
    pre = total / degree + bias_ref[...]
    sigma = jax.nn.sigmoid(pre)
    hidden = (pre * sigma).astype(bf16)
    hidden_ref[...] = jnp.where(first, hidden[:TILE], hidden[TILE:])
    hidden_other_ref[...] = jnp.where(first, hidden[TILE:], hidden[:TILE])
    up_mine = jnp.where(first, up_ref[:, :HALF], up_ref[:, HALF:])
    up_other = up_other_ref[...]
    up = jnp.concatenate(
        [jnp.where(first, up_mine, up_other), jnp.where(first, up_other, up_mine)], axis=0
    )
    grad_pre = up.astype(f32) * sigma * (1.0 + pre * (1.0 - sigma))
    scaled = (grad_pre / degree).astype(bf16).reshape(2, TILE, HALF)
    scaled_ref[...] = scaled
    for k in range(RUN):
        copies_ref[k] = scaled
    bias_out_ref[...] = jnp.sum(grad_pre, axis=0, keepdims=True)


def forward_math(ids, counts, total, degree, bias, upstream, up_other, pieces):
    return pl.pallas_call(
        forward_kernel,
        in_specs=[SMEM_SPEC] + [VMEM_SPEC] * (5 + PIECES),
        out_shape=(
            jax.ShapeDtypeStruct((TILE, HALF), bf16),
            jax.ShapeDtypeStruct((TILE, HALF), bf16),
            jax.ShapeDtypeStruct((RUN, 2, TILE, HALF), bf16),
            jax.ShapeDtypeStruct((2, TILE, HALF), bf16),
            jax.ShapeDtypeStruct((1, HALF), f32),
        ),
        name="forward_math",
    )(ids, counts, total, degree, bias, upstream, up_other, *pieces)


def backward_kernel(ids_ref, counts_ref, total_ref, bias_ref, feats_ref, feats_other_ref, *refs):
    pieces = (None,) + refs[: PIECES - 1]
    own_ref, other_ref, slab_ref, round_ref = refs[PIECES - 1 :]
    run, core = ids_ref[1], ids_ref[2]
    group = MEMBERS * TILE
    total = total_ref[...]
    for reach in (0, 2):
        rows = [block_of(ids_ref, pieces, reach, member) for member in range(MEMBERS)]
        total = total + jnp.dot(
            counts_ref[:, reach * group : reach * group + group],
            jnp.concatenate(rows, axis=0),
            preferred_element_type=f32,
        )
    round_ref[...] = total.astype(bf16).reshape(MEMBERS, TILE, HALF)
    own_ref[...] = round_ref[run * 2 + core]
    other_ref[...] = round_ref[run * 2 + 1 - core]
    part = jnp.zeros((F_RUN, HALF), f32)
    for feats, side in ((feats_ref, core), (feats_other_ref, 1 - core)):
        for k in range(RUN):
            part = part + jnp.dot(
                feats[k], round_ref[k * 2 + side], preferred_element_type=f32
            )
    part = part.astype(bf16)
    for row in range(F_RUN // 16):
        for lane in range(2):
            slab_ref[row * 2 + lane] = part[row * 16 : row * 16 + 16, lane * 128 : lane * 128 + 128]
    slab_ref[BIAS_SLAB] = bias_ref[...]
    for rest in range(BIAS_SLAB + 1, SLABS):
        slab_ref[rest] = jnp.zeros((16, 128), bf16)


def backward_math(ids, counts, total, bias_rows, feats, feats_other, pieces):
    return pl.pallas_call(
        backward_kernel,
        in_specs=[SMEM_SPEC] + [VMEM_SPEC] * (4 + PIECES),
        out_shape=(
            jax.ShapeDtypeStruct((TILE, HALF), bf16),
            jax.ShapeDtypeStruct((TILE, HALF), bf16),
            jax.ShapeDtypeStruct((SLABS, 16, 128), bf16),
        ),
        scratch_shapes=[pltpu.VMEM((MEMBERS, TILE, HALF), bf16)],
        name="backward_math",
    )(ids, counts, total, bias_rows, feats, feats_other, *pieces)


def assemble_kernel(ids_ref, mine_ref, other_ref, weight_ref, bias_ref):
    first = ids_ref[2] == 0
    bias = [jnp.zeros((2, 128), f32), jnp.zeros((2, 128), f32)]
    for x in range(4):
        for column in range(64):
            yh, run, z = column // 32, (column // 8) % 4, column % 8
            slab = (yh * 4 + x) * 8 + z
            if slab > BIAS_SLAB:
                continue
            mine, other = mine_ref[x, column], other_ref[x, column]
            for core in range(2):
                keep = first if core == 0 else jnp.logical_not(first)
                value = jnp.where(keep, mine, other)
                if slab == BIAS_SLAB:
                    rows = value.astype(f32)
                    bias[core] = bias[core] + (rows[:2] + rows[2:4])
                else:
                    row, lane = run * F_RUN + (slab // 2) * 16, core * HALF + (slab % 2) * 128
                    weight_ref[row : row + 16, lane : lane + 128] = value
    bias_ref[:2, :] = bias[0]
    bias_ref[2:, :] = bias[1]


def assemble(ids, mine, other):
    return pl.pallas_call(
        assemble_kernel,
        in_specs=[SMEM_SPEC] + [VMEM_SPEC] * 2,
        out_shape=(
            jax.ShapeDtypeStruct((RUN * F_RUN, HID), bf16),
            jax.ShapeDtypeStruct((4, 128), f32),
        ),
        name="assemble",
    )(ids, mine, other)


def high_low(value):
    high = lax.reduce_precision(value, 8, 7)
    return jnp.concatenate([high, value - high, jnp.zeros((12, 128), f32)], axis=0).astype(bf16)


def on_device(features, weight, bias, tile_cols, tile_count, nbr_slot, nbr_col, nbr_keep, upstream):
    group = (lax.axis_index("yh") * 4 + lax.axis_index("x")) * 8 + lax.axis_index("z")
    core = lax.axis_index("c")
    first = core == 0
    far_low, far_high = group % 32 == 0, group % 32 == 31
    ids = jnp.stack([group, lax.axis_index("yl"), core, far_low, far_high]).astype(i32)

    copies, same, cross = project(
        ids, tile_count, tile_cols, nbr_slot.T, nbr_col.T, nbr_keep.T, features, weight
    )
    straight, turned = across(same, cross)
    own = lax.all_to_all(copies, ("yl", "c"), 0, 0)
    tied, _ = lax.optimization_barrier((upstream, copies))
    up_other = swap_core(jnp.where(first, tied[:, HALF:], tied[:, :HALF]))
    slices = features.T.reshape(RUN, F_RUN, TILE)
    own, up_other, slices = lax.optimization_barrier((own, up_other, slices))
    straight, turned, _ = lax.optimization_barrier((straight, turned, own))
    received = jnp.stack([jnp.where(first, straight, turned), jnp.where(first, turned, straight)])
    low, high = neighbours(own)
    parts = along_run(received)
    counts, degree = forward_counts(ids, own)
    feats = lax.all_to_all(slices, "yl", 0, 0)
    feats_other = swap_core(feats)
    pieces = (own, low, high) + parts
    bias_half = jnp.where(first, bias[:HALF], bias[HALF:])[None]
    hidden_mine, hidden_send, scaled_copies, scaled, bias_part = forward_math(
        ids, counts, forward_own(ids, counts, own), degree, bias_half, upstream, up_other,
        pieces[1:],
    )

    received = across(scaled, None)
    own = lax.all_to_all(scaled_copies, "yl", 0, 0)
    hidden_got = swap_core(hidden_send)
    counts_back = backward_counts(ids, pieces)
    received, own, counts_back = lax.optimization_barrier((received, own, counts_back))
    own = own.reshape(MEMBERS, TILE, HALF)
    low, high = neighbours(own)
    parts = along_run(received)
    round_mine, round_send, slabs = backward_math(
        ids, counts_back, backward_own(counts_back, own), high_low(bias_part.reshape(2, 128)),
        feats, feats_other, (low, high) + parts,
    )
    round_got = swap_core(round_send)
    own_round = jnp.where(
        first,
        jnp.concatenate([round_mine, round_got], axis=1),
        jnp.concatenate([round_got, round_mine], axis=1),
    )
    grad_features = lax.dot_general(
        own_round, weight, (((1,), (1,)), ((), ())), preferred_element_type=f32
    ).astype(bf16)
    hidden = jnp.where(
        first,
        jnp.concatenate([hidden_mine, hidden_got], axis=1),
        jnp.concatenate([hidden_got, hidden_mine], axis=1),
    )
    terms = lax.all_to_all(slabs, WIDE, 0, 0)
    terms, grad_features, hidden = lax.optimization_barrier((terms, grad_features, hidden))
    reduced = jnp.sum(terms.astype(f32), axis=0)
    piece = jnp.where(
        group == BIAS_SLAB, high_low(reduced[:2] + reduced[2:4]), reduced.astype(bf16)
    )
    column = spread_to(piece, ("yh", "yl", "z"), 64)
    plane = spread_to(column, "x", 4)
    weight_grad, bias_grad = assemble(ids, plane, swap_core(plane))
    return hidden, grad_features, weight_grad, bias_grad.reshape(HID)


def solution(mesh):
    split = Mesh(mesh.devices.reshape(SIZES), AXES)
    rows = P(AXES, None)
    in_specs = (rows, P(), P(), rows, P(AXES), rows, rows, rows, rows)
    out_specs = (rows, rows, P(), P())
    return jax.shard_map(
        on_device, mesh=split, in_specs=in_specs, out_specs=out_specs, check_vma=False
    )
```

```python
import jax
import jax.numpy as jnp
from jax import lax
from jax.experimental import pallas as pl
from jax.experimental.pallas import tpu as pltpu
from jax.sharding import Mesh
from jax.sharding import PartitionSpec as P

TILE = 128
KNN = 15
KEYS = 16
HID = 512
HALF = 256
AXES = ("yh", "x", "z", "yl", "c")
SIZES = (2, 4, 8, 4, 2)
WIDE = ("yh", "x", "z")
GROUPS = 64
RUN = 4
MEMBERS = 8
REACH = 3
PIECES = 7
WINDOW = REACH * MEMBERS * TILE
BLOCKS = 512
DEAD = 31
F_RUN = 448
SLABS = 64
BIAS_SLAB = 56

i32 = jnp.int32
bf16 = jnp.bfloat16
f32 = jnp.float32

EAGER = pl.CostEstimate(flops=4_000_000_000, transcendentals=0, bytes_accessed=8_000_000)
SMEM_SPEC = pl.BlockSpec(memory_space=pltpu.SMEM)
VMEM_SPEC = pl.BlockSpec(memory_space=pltpu.VMEM)


def spread_to(shard, axes, count):
    return lax.all_to_all(jnp.broadcast_to(shard[None], (count,) + shard.shape), axes, 0, 0)


FAR = ((31, 32), (63, 0), (32, 31), (0, 63))


def device(group, run, core):
    return (group * RUN + run) * 2 + core


def across(same, cross):
    pairs = [(a, b, r, c) for a, b in FAR for r in range(RUN) for c in range(2)]
    straight = [(device(a, r, c), device(b, 3 - r, c)) for a, b, r, c in pairs]
    turned = [(device(a, r, c), device(b, 3 - r, 1 - c)) for a, b, r, c in pairs]
    got = lax.ppermute(same, AXES, straight)
    return got if cross is None else (got, lax.ppermute(cross, AXES, turned))


def along_run(block):
    parts = [block]
    for step in range(1, RUN):
        pairs = [
            (device(a, r, c), device(a, r ^ step, c))
            for a, _ in FAR for r in range(RUN) for c in range(2)
        ]
        parts.append(lax.ppermute(block, AXES, pairs))
    return tuple(parts)


def block_of(ids_ref, pieces, reach, member):
    own, low, high = pieces[:REACH]
    if reach == 1:
        return own[member, :TILE, :]
    near = (low, high)[reach // 2][member, :TILE, :]
    far = pieces[REACH + member // 2][member % 2, :TILE, :]
    return jnp.where(ids_ref[3 + reach // 2] > 0, far, near)


def keys_of(ids_ref, pieces, reach, member):
    own, low, high = pieces[:REACH]
    if reach == 1:
        return own[member, TILE:, :].astype(f32)
    near = (low, high)[reach // 2][member, TILE:, :].astype(f32)
    far = pieces[REACH + member // 2][member % 2, TILE:, :].astype(f32)
    return jnp.where(ids_ref[3 + reach // 2] > 0, far, near)


def neighbours(block):
    forward = [(i, (i + 1) % GROUPS) for i in range(GROUPS) if i % 32 != 31]
    backward = [(target, source) for source, target in forward]
    return lax.ppermute(block, WIDE, forward), lax.ppermute(block, WIDE, backward)


def swap_core(block):
    return lax.ppermute(block, "c", [(0, 1), (1, 0)])


def project_kernel(ids_ref, count_ref, tiles_ref, slot_ref, col_ref, keep_ref, features_ref, weight_ref,
                   copies_ref, same_ref, cross_ref):
    base = (ids_ref[0] - 1) * MEMBERS
    slot = slot_ref[...]
    live = keep_ref[...] * (slot < count_ref[0]).astype(i32)
    position = jnp.zeros_like(slot)
    for k in range(tiles_ref.shape[1]):
        block = tiles_ref[0, k] - base
        block = jnp.where(block < 0, block + BLOCKS, block)
        block = jnp.where(block >= BLOCKS, block - BLOCKS, block)
        position = position + jnp.where(slot == k, block, 0)
    pad = jnp.zeros((KEYS - KNN, TILE), i32)

    def rows(value):
        return jnp.concatenate([value, pad], axis=0)

    dead = rows(1 - live) + lax.broadcasted_iota(i32, (KEYS, TILE), 0) // KNN
    blocks = jnp.where(dead > 0, DEAD, rows(position))
    keys = jnp.concatenate([blocks, rows(col_ref[...])], axis=1).astype(f32).astype(bf16)
    projected = jnp.dot(features_ref[...], weight_ref[...], preferred_element_type=f32).astype(bf16)
    for k in range(MEMBERS):
        half = (k % 2) * HALF
        copies_ref[k, :TILE, :] = projected[:, half : half + HALF]
        copies_ref[k, TILE:, :] = keys
    first = ids_ref[2] == 0
    left, right = projected[:, :HALF], projected[:, HALF:]
    same_ref[:TILE, :] = jnp.where(first, left, right)
    same_ref[TILE:, :] = keys
    cross_ref[:TILE, :] = jnp.where(first, right, left)
    cross_ref[TILE:, :] = keys


def project(ids, tile_count, tile_cols, slot, col, keep, features, weight):
    return pl.pallas_call(
        project_kernel,
        in_specs=[SMEM_SPEC] * 3 + [VMEM_SPEC] * 5,
        out_shape=(
            jax.ShapeDtypeStruct((MEMBERS, TILE + KEYS, HALF), bf16),
            jax.ShapeDtypeStruct((TILE + KEYS, HALF), bf16),
            jax.ShapeDtypeStruct((TILE + KEYS, HALF), bf16),
        ),
        name="project",
    )(ids, tile_count, tile_cols, slot, col, keep, features, weight)


def digits_of(block, wanted):
    valid = lax.shift_right_arithmetic(block, 3) == wanted
    shift = 4 * jnp.bitwise_and(block, 7)
    return jnp.where(valid, lax.shift_left(jnp.ones_like(shift), shift), 0)


def forward_counts_kernel(ids_ref, own_ref, counts_ref, degree_ref):
    run = ids_ref[1]
    for core in range(2):
        keys = own_ref[run * 2 + core, TILE:, :].astype(f32).astype(i32).T
        block, cells = keys[:TILE, :], keys[TILE:, :]
        live = jnp.where(block < DEAD, 1.0, 0.0)
        degree_ref[core * TILE : core * TILE + TILE, :] = 1.0 + jnp.sum(live, axis=1, keepdims=True)
        reach_of = lax.shift_right_logical(block, 3)
        turn = jnp.bitwise_xor(run, 3) * 2
        low_twist = jnp.where(reach_of == 0, ids_ref[3] * turn, 0)
        twist = low_twist + jnp.where(reach_of == 2, ids_ref[4] * turn, 0)
        block = jnp.bitwise_xor(block, twist)
        digits = [digits_of(block, reach) for reach in range(REACH)]
        lanes = lax.broadcasted_iota(i32, (16, 128), 1)
        for step in range(TILE // 16):
            here = slice(step * 16, step * 16 + 16)
            totals = [jnp.zeros((16, 128), i32) for _ in range(REACH)]
            for e in range(KNN):
                hit = cells[here, e : e + 1] == lanes
                for reach in range(REACH):
                    totals[reach] = totals[reach] + jnp.where(hit, digits[reach][here, e : e + 1], 0)
            row = core * TILE + step * 16
            for tile in range(REACH * MEMBERS):
                digit = lax.shift_right_logical(totals[tile // 8], 4 * (tile % 8))
                count = jnp.bitwise_and(digit, 15).astype(f32).astype(bf16)
                counts_ref[row : row + 16, tile * 128 : tile * 128 + 128] = count


def forward_counts(ids, own):
    return pl.pallas_call(
        forward_counts_kernel,
        in_specs=[SMEM_SPEC, VMEM_SPEC],
        out_shape=(
            jax.ShapeDtypeStruct((2 * TILE, WINDOW), bf16),
            jax.ShapeDtypeStruct((2 * TILE, 1), f32),
        ),
        cost_estimate=EAGER,
        name="forward_counts",
    )(ids, own)


def backward_counts_kernel(ids_ref, *refs):
    pieces, out_ref = refs[:PIECES], refs[PIECES]
    for member in range(MEMBERS):
        for reach in range(REACH):
            keys = keys_of(ids_ref, pieces, reach, member).astype(i32)
            digits = digits_of(keys[:, :TILE], REACH - 1 - reach)
            cells = keys[:, TILE:]
            lane = (reach * MEMBERS + member) * TILE
            for step in range(TILE // 16):
                rows = lax.broadcasted_iota(i32, (16, 128), 0) + step * 16
                total = jnp.zeros((16, 128), i32)
                for e in range(KNN):
                    total = total + jnp.where(cells[e : e + 1, :] == rows, digits[e : e + 1, :], 0)
                for k in range(MEMBERS):
                    count = jnp.bitwise_and(lax.shift_right_logical(total, 4 * k), 15)
                    at = k * TILE + step * 16
                    out_ref[at : at + 16, lane : lane + TILE] = count.astype(f32).astype(bf16)


def backward_counts(ids, pieces):
    return pl.pallas_call(
        backward_counts_kernel,
        in_specs=[SMEM_SPEC] + [VMEM_SPEC] * PIECES,
        out_shape=jax.ShapeDtypeStruct((MEMBERS * TILE, WINDOW), bf16),
        cost_estimate=EAGER,
        name="backward_counts",
    )(ids, *pieces)


def forward_own_kernel(ids_ref, counts_ref, own_ref, total_ref):
    run = ids_ref[1]
    total = jnp.concatenate(
        [own_ref[run * 2 + core, :TILE, :].astype(f32) for core in range(2)], axis=0
    )
    for member in range(MEMBERS):
        lane = (MEMBERS + member) * TILE
        total = total + jnp.dot(
            counts_ref[:, lane : lane + TILE],
            own_ref[member, :TILE, :],
            preferred_element_type=f32,
        )
    total_ref[...] = total


def forward_own(ids, counts, own):
    return pl.pallas_call(
        forward_own_kernel,
        in_specs=[SMEM_SPEC] + [VMEM_SPEC] * 2,
        out_shape=jax.ShapeDtypeStruct((2 * TILE, HALF), f32),
        cost_estimate=EAGER,
        name="forward_own",
    )(ids, counts, own)


def backward_own_kernel(counts_ref, own_ref, total_ref):
    group = MEMBERS * TILE
    own = own_ref[...].reshape(group, HALF)
    total_ref[...] = own.astype(f32) + jnp.dot(
        counts_ref[:, group : 2 * group], own, preferred_element_type=f32
    )


def backward_own(counts, own):
    return pl.pallas_call(
        backward_own_kernel,
        in_specs=[VMEM_SPEC] * 2,
        out_shape=jax.ShapeDtypeStruct((MEMBERS * TILE, HALF), f32),
        cost_estimate=EAGER,
        name="backward_own",
    )(counts, own)


def forward_kernel(
    ids_ref, counts_ref, total_ref, degree_ref, bias_ref, up_ref, up_other_ref, *refs
):
    pieces = (None,) + refs[: PIECES - 1]
    hidden_ref, hidden_other_ref, copies_ref, scaled_ref, bias_out_ref = refs[PIECES - 1 :]
    first = ids_ref[2] == 0
    total = total_ref[...]
    for reach in (0, 2):
        for member in range(MEMBERS):
            lane = (reach * MEMBERS + member) * TILE
            total = total + jnp.dot(
                counts_ref[:, lane : lane + TILE],
                block_of(ids_ref, pieces, reach, member),
                preferred_element_type=f32,
            )
    degree = degree_ref[...]
    pre = total / degree + bias_ref[...]
    sigma = jax.nn.sigmoid(pre)
    hidden = (pre * sigma).astype(bf16)
    hidden_ref[...] = jnp.where(first, hidden[:TILE], hidden[TILE:])
    hidden_other_ref[...] = jnp.where(first, hidden[TILE:], hidden[:TILE])
    up_mine = jnp.where(first, up_ref[:, :HALF], up_ref[:, HALF:])
    up_other = up_other_ref[...]
    up = jnp.concatenate(
        [jnp.where(first, up_mine, up_other), jnp.where(first, up_other, up_mine)], axis=0
    )
    grad_pre = up.astype(f32) * sigma * (1.0 + pre * (1.0 - sigma))
    scaled = (grad_pre / degree).astype(bf16).reshape(2, TILE, HALF)
    scaled_ref[...] = scaled
    for k in range(RUN):
        copies_ref[k] = scaled
    bias_out_ref[...] = jnp.sum(grad_pre, axis=0, keepdims=True)


def forward_math(ids, counts, total, degree, bias, upstream, up_other, pieces):
    return pl.pallas_call(
        forward_kernel,
        in_specs=[SMEM_SPEC] + [VMEM_SPEC] * (5 + PIECES),
        out_shape=(
            jax.ShapeDtypeStruct((TILE, HALF), bf16),
            jax.ShapeDtypeStruct((TILE, HALF), bf16),
            jax.ShapeDtypeStruct((RUN, 2, TILE, HALF), bf16),
            jax.ShapeDtypeStruct((2, TILE, HALF), bf16),
            jax.ShapeDtypeStruct((1, HALF), f32),
        ),
        name="forward_math",
    )(ids, counts, total, degree, bias, upstream, up_other, *pieces)


def backward_kernel(ids_ref, counts_ref, total_ref, bias_ref, feats_ref, feats_other_ref, *refs):
    pieces = (None,) + refs[: PIECES - 1]
    own_ref, other_ref, slab_ref, round_ref = refs[PIECES - 1 :]
    run, core = ids_ref[1], ids_ref[2]
    group = MEMBERS * TILE
    total = total_ref[...]
    for reach in (0, 2):
        rows = [block_of(ids_ref, pieces, reach, member) for member in range(MEMBERS)]
        total = total + jnp.dot(
            counts_ref[:, reach * group : reach * group + group],
            jnp.concatenate(rows, axis=0),
            preferred_element_type=f32,
        )
    round_ref[...] = total.astype(bf16).reshape(MEMBERS, TILE, HALF)
    own_ref[...] = round_ref[run * 2 + core]
    other_ref[...] = round_ref[run * 2 + 1 - core]
    part = jnp.zeros((F_RUN, HALF), f32)
    for feats, side in ((feats_ref, core), (feats_other_ref, 1 - core)):
        part = part + jnp.dot(
            jnp.concatenate([feats[k] for k in range(RUN)], axis=1),
            jnp.concatenate([round_ref[k * 2 + side] for k in range(RUN)], axis=0),
            preferred_element_type=f32,
        )
    part = part.astype(bf16)
    for row in range(F_RUN // 16):
        for lane in range(2):
            slab_ref[row * 2 + lane] = part[row * 16 : row * 16 + 16, lane * 128 : lane * 128 + 128]
    slab_ref[BIAS_SLAB] = bias_ref[...]
    for rest in range(BIAS_SLAB + 1, SLABS):
        slab_ref[rest] = jnp.zeros((16, 128), bf16)


def backward_math(ids, counts, total, bias_rows, feats, feats_other, pieces):
    return pl.pallas_call(
        backward_kernel,
        in_specs=[SMEM_SPEC] + [VMEM_SPEC] * (4 + PIECES),
        out_shape=(
            jax.ShapeDtypeStruct((TILE, HALF), bf16),
            jax.ShapeDtypeStruct((TILE, HALF), bf16),
            jax.ShapeDtypeStruct((SLABS, 16, 128), bf16),
        ),
        scratch_shapes=[pltpu.VMEM((MEMBERS, TILE, HALF), bf16)],
        name="backward_math",
    )(ids, counts, total, bias_rows, feats, feats_other, *pieces)


def assemble_kernel(ids_ref, mine_ref, other_ref, weight_ref, bias_ref):
    first = ids_ref[2] == 0
    bias = [jnp.zeros((2, 128), f32), jnp.zeros((2, 128), f32)]
    for x in range(4):
        for column in range(64):
            yh, run, z = column // 32, (column // 8) % 4, column % 8
            slab = (yh * 4 + x) * 8 + z
            if slab > BIAS_SLAB:
                continue
            mine, other = mine_ref[x, column], other_ref[x, column]
            for core in range(2):
                keep = first if core == 0 else jnp.logical_not(first)
                value = jnp.where(keep, mine, other)
                if slab == BIAS_SLAB:
                    rows = value.astype(f32)
                    bias[core] = bias[core] + (rows[:2] + rows[2:4])
                else:
                    row, lane = run * F_RUN + (slab // 2) * 16, core * HALF + (slab % 2) * 128
                    weight_ref[row : row + 16, lane : lane + 128] = value
    bias_ref[:2, :] = bias[0]
    bias_ref[2:, :] = bias[1]


def assemble(ids, mine, other):
    return pl.pallas_call(
        assemble_kernel,
        in_specs=[SMEM_SPEC] + [VMEM_SPEC] * 2,
        out_shape=(
            jax.ShapeDtypeStruct((RUN * F_RUN, HID), bf16),
            jax.ShapeDtypeStruct((4, 128), f32),
        ),
        name="assemble",
    )(ids, mine, other)


def high_low(value):
    high = lax.reduce_precision(value, 8, 7)
    return jnp.concatenate([high, value - high, jnp.zeros((12, 128), f32)], axis=0).astype(bf16)


def on_device(features, weight, bias, tile_cols, tile_count, nbr_slot, nbr_col, nbr_keep, upstream):
    group = (lax.axis_index("yh") * 4 + lax.axis_index("x")) * 8 + lax.axis_index("z")
    core = lax.axis_index("c")
    first = core == 0
    far_low, far_high = group % 32 == 0, group % 32 == 31
    ids = jnp.stack([group, lax.axis_index("yl"), core, far_low, far_high]).astype(i32)

    copies, same, cross = project(
        ids, tile_count, tile_cols, nbr_slot.T, nbr_col.T, nbr_keep.T, features, weight
    )
    straight, turned = across(same, cross)
    own = lax.all_to_all(copies, ("yl", "c"), 0, 0)
    tied, _ = lax.optimization_barrier((upstream, copies))
    up_other = swap_core(jnp.where(first, tied[:, HALF:], tied[:, :HALF]))
    slices = features.T.reshape(RUN, F_RUN, TILE)
    own, up_other, slices = lax.optimization_barrier((own, up_other, slices))
    straight, turned, _ = lax.optimization_barrier((straight, turned, own))
    received = jnp.stack([jnp.where(first, straight, turned), jnp.where(first, turned, straight)])
    low, high = neighbours(own)
    parts = along_run(received)
    counts, degree = forward_counts(ids, own)
    feats = lax.all_to_all(slices, "yl", 0, 0)
    feats_other = swap_core(feats)
    pieces = (own, low, high) + parts
    bias_half = jnp.where(first, bias[:HALF], bias[HALF:])[None]
    hidden_mine, hidden_send, scaled_copies, scaled, bias_part = forward_math(
        ids, counts, forward_own(ids, counts, own), degree, bias_half, upstream, up_other,
        pieces[1:],
    )

    received = across(scaled, None)
    own = lax.all_to_all(scaled_copies, "yl", 0, 0)
    hidden_got = swap_core(hidden_send)
    counts_back = backward_counts(ids, pieces)
    received, own, counts_back = lax.optimization_barrier((received, own, counts_back))
    own = own.reshape(MEMBERS, TILE, HALF)
    low, high = neighbours(own)
    parts = along_run(received)
    round_mine, round_send, slabs = backward_math(
        ids, counts_back, backward_own(counts_back, own), high_low(bias_part.reshape(2, 128)),
        feats, feats_other, (low, high) + parts,
    )
    round_got = swap_core(round_send)
    own_round = jnp.where(
        first,
        jnp.concatenate([round_mine, round_got], axis=1),
        jnp.concatenate([round_got, round_mine], axis=1),
    )
    grad_features = lax.dot_general(
        own_round, weight, (((1,), (1,)), ((), ())), preferred_element_type=f32
    ).astype(bf16)
    hidden = jnp.where(
        first,
        jnp.concatenate([hidden_mine, hidden_got], axis=1),
        jnp.concatenate([hidden_got, hidden_mine], axis=1),
    )
    terms = lax.all_to_all(slabs, WIDE, 0, 0)
    terms, grad_features, hidden = lax.optimization_barrier((terms, grad_features, hidden))
    reduced = jnp.sum(terms.astype(f32), axis=0)
    piece = jnp.where(
        group == BIAS_SLAB, high_low(reduced[:2] + reduced[2:4]), reduced.astype(bf16)
    )
    column = spread_to(piece, ("yh", "yl", "z"), 64)
    plane = spread_to(column, "x", 4)
    weight_grad, bias_grad = assemble(ids, plane, swap_core(plane))
    return hidden, grad_features, weight_grad, bias_grad.reshape(HID)


def solution(mesh):
    split = Mesh(mesh.devices.reshape(SIZES), AXES)
    rows = P(AXES, None)
    in_specs = (rows, P(), P(), rows, P(AXES), rows, rows, rows, rows)
    out_specs = (rows, rows, P(), P())
    return jax.shard_map(
        on_device, mesh=split, in_specs=in_specs, out_specs=out_specs, check_vma=False
    )
```

```python
import jax
import jax.numpy as jnp
from jax import lax
from jax.experimental import pallas as pl
from jax.experimental.pallas import tpu as pltpu
from jax.sharding import Mesh
from jax.sharding import PartitionSpec as P

TILE = 128
KNN = 15
KEYS = 16
HID = 512
HALF = 256
AXES = ("yh", "x", "z", "yl", "c")
SIZES = (2, 4, 8, 4, 2)
WIDE = ("yh", "x", "z")
GROUPS = 64
RUN = 4
MEMBERS = 8
REACH = 3
PIECES = 7
WINDOW = REACH * MEMBERS * TILE
BLOCKS = 512
DEAD = 31
F_RUN = 448
SLABS = 64
BIAS_SLAB = 56

i32 = jnp.int32
bf16 = jnp.bfloat16
f32 = jnp.float32

EAGER = pl.CostEstimate(flops=4_000_000_000, transcendentals=0, bytes_accessed=8_000_000)
SMEM_SPEC = pl.BlockSpec(memory_space=pltpu.SMEM)
VMEM_SPEC = pl.BlockSpec(memory_space=pltpu.VMEM)


def spread_to(shard, axes, count):
    return lax.all_to_all(jnp.broadcast_to(shard[None], (count,) + shard.shape), axes, 0, 0)


FAR = ((31, 32), (63, 0), (32, 31), (0, 63))


def device(group, run, core):
    return (group * RUN + run) * 2 + core


def across(same, cross):
    pairs = [(a, b, r, c) for a, b in FAR for r in range(RUN) for c in range(2)]
    straight = [(device(a, r, c), device(b, 3 - r, c)) for a, b, r, c in pairs]
    turned = [(device(a, r, c), device(b, 3 - r, 1 - c)) for a, b, r, c in pairs]
    got = lax.ppermute(same, AXES, straight)
    return got if cross is None else (got, lax.ppermute(cross, AXES, turned))


def along_run(block):
    parts = [block]
    for step in range(1, RUN):
        pairs = [
            (device(a, r, c), device(a, r ^ step, c))
            for a, _ in FAR for r in range(RUN) for c in range(2)
        ]
        parts.append(lax.ppermute(block, AXES, pairs))
    return tuple(parts)


def block_of(ids_ref, pieces, reach, member):
    own, low, high = pieces[:REACH]
    if reach == 1:
        return own[member, :TILE, :]
    near = (low, high)[reach // 2][member, :TILE, :]
    far = pieces[REACH + member // 2][member % 2, :TILE, :]
    return jnp.where(ids_ref[3 + reach // 2] > 0, far, near)


def keys_of(ids_ref, pieces, reach, member):
    own, low, high = pieces[:REACH]
    if reach == 1:
        return own[member, TILE:, :].astype(f32)
    near = (low, high)[reach // 2][member, TILE:, :].astype(f32)
    far = pieces[REACH + member // 2][member % 2, TILE:, :].astype(f32)
    return jnp.where(ids_ref[3 + reach // 2] > 0, far, near)


def neighbours(block):
    forward = [(i, (i + 1) % GROUPS) for i in range(GROUPS) if i % 32 != 31]
    backward = [(target, source) for source, target in forward]
    return lax.ppermute(block, WIDE, forward), lax.ppermute(block, WIDE, backward)


def swap_core(block):
    return lax.ppermute(block, "c", [(0, 1), (1, 0)])


def project_kernel(ids_ref, count_ref, tiles_ref, slot_ref, col_ref, keep_ref, features_ref, weight_ref,
                   copies_ref, same_ref, cross_ref):
    base = (ids_ref[0] - 1) * MEMBERS
    slot = slot_ref[...]
    live = keep_ref[...] * (slot < count_ref[0]).astype(i32)
    position = jnp.zeros_like(slot)
    for k in range(tiles_ref.shape[1]):
        block = tiles_ref[0, k] - base
        block = jnp.where(block < 0, block + BLOCKS, block)
        block = jnp.where(block >= BLOCKS, block - BLOCKS, block)
        position = position + jnp.where(slot == k, block, 0)
    pad = jnp.zeros((KEYS - KNN, TILE), i32)

    def rows(value):
        return jnp.concatenate([value, pad], axis=0)

    dead = rows(1 - live) + lax.broadcasted_iota(i32, (KEYS, TILE), 0) // KNN
    blocks = jnp.where(dead > 0, DEAD, rows(position))
    keys = jnp.concatenate([blocks, rows(col_ref[...])], axis=1).astype(f32).astype(bf16)
    projected = jnp.dot(features_ref[...], weight_ref[...], preferred_element_type=f32).astype(bf16)
    for k in range(MEMBERS):
        half = (k % 2) * HALF
        copies_ref[k, :TILE, :] = projected[:, half : half + HALF]
        copies_ref[k, TILE:, :] = keys
    first = ids_ref[2] == 0
    left, right = projected[:, :HALF], projected[:, HALF:]
    same_ref[:TILE, :] = jnp.where(first, left, right)
    same_ref[TILE:, :] = keys
    cross_ref[:TILE, :] = jnp.where(first, right, left)
    cross_ref[TILE:, :] = keys


def project(ids, tile_count, tile_cols, slot, col, keep, features, weight):
    return pl.pallas_call(
        project_kernel,
        in_specs=[SMEM_SPEC] * 3 + [VMEM_SPEC] * 5,
        out_shape=(
            jax.ShapeDtypeStruct((MEMBERS, TILE + KEYS, HALF), bf16),
            jax.ShapeDtypeStruct((TILE + KEYS, HALF), bf16),
            jax.ShapeDtypeStruct((TILE + KEYS, HALF), bf16),
        ),
        name="project",
    )(ids, tile_count, tile_cols, slot, col, keep, features, weight)


def digits_of(block, wanted):
    valid = lax.shift_right_arithmetic(block, 3) == wanted
    shift = 4 * jnp.bitwise_and(block, 7)
    return jnp.where(valid, lax.shift_left(jnp.ones_like(shift), shift), 0)


def forward_counts_kernel(ids_ref, own_ref, counts_ref, degree_ref):
    run = ids_ref[1]
    for core in range(2):
        keys = own_ref[run * 2 + core, TILE:, :].astype(f32).astype(i32).T
        block, cells = keys[:TILE, :], keys[TILE:, :]
        live = jnp.where(block < DEAD, 1.0, 0.0)
        degree_ref[core * TILE : core * TILE + TILE, :] = 1.0 + jnp.sum(live, axis=1, keepdims=True)
        reach_of = lax.shift_right_logical(block, 3)
        turn = jnp.bitwise_xor(run, 3) * 2
        low_twist = jnp.where(reach_of == 0, ids_ref[3] * turn, 0)
        twist = low_twist + jnp.where(reach_of == 2, ids_ref[4] * turn, 0)
        block = jnp.bitwise_xor(block, twist)
        digits = [digits_of(block, reach) for reach in range(REACH)]
        lanes = lax.broadcasted_iota(i32, (16, 128), 1)
        for step in range(TILE // 16):
            here = slice(step * 16, step * 16 + 16)
            totals = [jnp.zeros((16, 128), i32) for _ in range(REACH)]
            for e in range(KNN):
                hit = cells[here, e : e + 1] == lanes
                for reach in range(REACH):
                    totals[reach] = totals[reach] + jnp.where(hit, digits[reach][here, e : e + 1], 0)
            row = core * TILE + step * 16
            for tile in range(REACH * MEMBERS):
                digit = lax.shift_right_logical(totals[tile // 8], 4 * (tile % 8))
                count = jnp.bitwise_and(digit, 15).astype(f32).astype(bf16)
                counts_ref[row : row + 16, tile * 128 : tile * 128 + 128] = count


def forward_counts(ids, own):
    return pl.pallas_call(
        forward_counts_kernel,
        in_specs=[SMEM_SPEC, VMEM_SPEC],
        out_shape=(
            jax.ShapeDtypeStruct((2 * TILE, WINDOW), bf16),
            jax.ShapeDtypeStruct((2 * TILE, 1), f32),
        ),
        cost_estimate=EAGER,
        name="forward_counts",
    )(ids, own)


def backward_counts_kernel(ids_ref, *refs):
    pieces, out_ref = refs[:PIECES], refs[PIECES]
    for member in range(MEMBERS):
        for reach in range(REACH):
            keys = keys_of(ids_ref, pieces, reach, member).astype(i32)
            digits = digits_of(keys[:, :TILE], REACH - 1 - reach)
            cells = keys[:, TILE:]
            lane = (reach * MEMBERS + member) * TILE
            for step in range(TILE // 16):
                rows = lax.broadcasted_iota(i32, (16, 128), 0) + step * 16
                total = jnp.zeros((16, 128), i32)
                for e in range(KNN):
                    total = total + jnp.where(cells[e : e + 1, :] == rows, digits[e : e + 1, :], 0)
                for k in range(MEMBERS):
                    count = jnp.bitwise_and(lax.shift_right_logical(total, 4 * k), 15)
                    at = k * TILE + step * 16
                    out_ref[at : at + 16, lane : lane + TILE] = count.astype(f32).astype(bf16)


def backward_counts(ids, pieces):
    return pl.pallas_call(
        backward_counts_kernel,
        in_specs=[SMEM_SPEC] + [VMEM_SPEC] * PIECES,
        out_shape=jax.ShapeDtypeStruct((MEMBERS * TILE, WINDOW), bf16),
        cost_estimate=EAGER,
        name="backward_counts",
    )(ids, *pieces)


def forward_own_kernel(ids_ref, counts_ref, own_ref, total_ref):
    run = ids_ref[1]
    total = jnp.concatenate(
        [own_ref[run * 2 + core, :TILE, :].astype(f32) for core in range(2)], axis=0
    )
    for member in range(MEMBERS):
        lane = (MEMBERS + member) * TILE
        total = total + jnp.dot(
            counts_ref[:, lane : lane + TILE],
            own_ref[member, :TILE, :],
            preferred_element_type=f32,
        )
    total_ref[...] = total


def forward_own(ids, counts, own):
    return pl.pallas_call(
        forward_own_kernel,
        in_specs=[SMEM_SPEC] + [VMEM_SPEC] * 2,
        out_shape=jax.ShapeDtypeStruct((2 * TILE, HALF), f32),
        name="forward_own",
    )(ids, counts, own)


def backward_own_kernel(counts_ref, own_ref, total_ref):
    group = MEMBERS * TILE
    own = own_ref[...].reshape(group, HALF)
    total_ref[...] = own.astype(f32) + jnp.dot(
        counts_ref[:, group : 2 * group], own, preferred_element_type=f32
    )


def backward_own(counts, own):
    return pl.pallas_call(
        backward_own_kernel,
        in_specs=[VMEM_SPEC] * 2,
        out_shape=jax.ShapeDtypeStruct((MEMBERS * TILE, HALF), f32),
        cost_estimate=EAGER,
        name="backward_own",
    )(counts, own)


def forward_kernel(
    ids_ref, counts_ref, total_ref, degree_ref, bias_ref, up_ref, up_other_ref, *refs
):
    pieces = (None,) + refs[: PIECES - 1]
    hidden_ref, hidden_other_ref, copies_ref, scaled_ref, bias_out_ref = refs[PIECES - 1 :]
    first = ids_ref[2] == 0
    total = total_ref[...]
    for reach in (0, 2):
        for member in range(MEMBERS):
            lane = (reach * MEMBERS + member) * TILE
            total = total + jnp.dot(
                counts_ref[:, lane : lane + TILE],
                block_of(ids_ref, pieces, reach, member),
                preferred_element_type=f32,
            )
    degree = degree_ref[...]
    pre = total / degree + bias_ref[...]
    sigma = jax.nn.sigmoid(pre)
    hidden = (pre * sigma).astype(bf16)
    hidden_ref[...] = jnp.where(first, hidden[:TILE], hidden[TILE:])
    hidden_other_ref[...] = jnp.where(first, hidden[TILE:], hidden[:TILE])
    up_mine = jnp.where(first, up_ref[:, :HALF], up_ref[:, HALF:])
    up_other = up_other_ref[...]
    up = jnp.concatenate(
        [jnp.where(first, up_mine, up_other), jnp.where(first, up_other, up_mine)], axis=0
    )
    grad_pre = up.astype(f32) * sigma * (1.0 + pre * (1.0 - sigma))
    scaled = (grad_pre / degree).astype(bf16).reshape(2, TILE, HALF)
    scaled_ref[...] = scaled
    for k in range(RUN):
        copies_ref[k] = scaled
    bias_out_ref[...] = jnp.sum(grad_pre, axis=0, keepdims=True)


def forward_math(ids, counts, total, degree, bias, upstream, up_other, pieces):
    return pl.pallas_call(
        forward_kernel,
        in_specs=[SMEM_SPEC] + [VMEM_SPEC] * (5 + PIECES),
        out_shape=(
            jax.ShapeDtypeStruct((TILE, HALF), bf16),
            jax.ShapeDtypeStruct((TILE, HALF), bf16),
            jax.ShapeDtypeStruct((RUN, 2, TILE, HALF), bf16),
            jax.ShapeDtypeStruct((2, TILE, HALF), bf16),
            jax.ShapeDtypeStruct((1, HALF), f32),
        ),
        name="forward_math",
    )(ids, counts, total, degree, bias, upstream, up_other, *pieces)


def backward_kernel(ids_ref, counts_ref, total_ref, bias_ref, feats_ref, feats_other_ref, *refs):
    pieces = (None,) + refs[: PIECES - 1]
    own_ref, other_ref, slab_ref, round_ref = refs[PIECES - 1 :]
    run, core = ids_ref[1], ids_ref[2]
    group = MEMBERS * TILE
    total = total_ref[...]
    for reach in (0, 2):
        rows = [block_of(ids_ref, pieces, reach, member) for member in range(MEMBERS)]
        total = total + jnp.dot(
            counts_ref[:, reach * group : reach * group + group],
            jnp.concatenate(rows, axis=0),
            preferred_element_type=f32,
        )
    round_ref[...] = total.astype(bf16).reshape(MEMBERS, TILE, HALF)
    own_ref[...] = round_ref[run * 2 + core]
    other_ref[...] = round_ref[run * 2 + 1 - core]
    part = jnp.zeros((F_RUN, HALF), f32)
    for feats, side in ((feats_ref, core), (feats_other_ref, 1 - core)):
        part = part + jnp.dot(
            jnp.concatenate([feats[k] for k in range(RUN)], axis=1),
            jnp.concatenate([round_ref[k * 2 + side] for k in range(RUN)], axis=0),
            preferred_element_type=f32,
        )
    part = part.astype(bf16)
    for row in range(F_RUN // 16):
        for lane in range(2):
            slab_ref[row * 2 + lane] = part[row * 16 : row * 16 + 16, lane * 128 : lane * 128 + 128]
    slab_ref[BIAS_SLAB] = bias_ref[...]
    for rest in range(BIAS_SLAB + 1, SLABS):
        slab_ref[rest] = jnp.zeros((16, 128), bf16)


def backward_math(ids, counts, total, bias_rows, feats, feats_other, pieces):
    return pl.pallas_call(
        backward_kernel,
        in_specs=[SMEM_SPEC] + [VMEM_SPEC] * (4 + PIECES),
        out_shape=(
            jax.ShapeDtypeStruct((TILE, HALF), bf16),
            jax.ShapeDtypeStruct((TILE, HALF), bf16),
            jax.ShapeDtypeStruct((SLABS, 16, 128), bf16),
        ),
        scratch_shapes=[pltpu.VMEM((MEMBERS, TILE, HALF), bf16)],
        name="backward_math",
    )(ids, counts, total, bias_rows, feats, feats_other, *pieces)


def assemble_kernel(ids_ref, mine_ref, other_ref, weight_ref, bias_ref):
    first = ids_ref[2] == 0
    bias = [jnp.zeros((2, 128), f32), jnp.zeros((2, 128), f32)]
    for x in range(4):
        for column in range(64):
            yh, run, z = column // 32, (column // 8) % 4, column % 8
            slab = (yh * 4 + x) * 8 + z
            if slab > BIAS_SLAB:
                continue
            mine, other = mine_ref[x, column], other_ref[x, column]
            for core in range(2):
                keep = first if core == 0 else jnp.logical_not(first)
                value = jnp.where(keep, mine, other)
                if slab == BIAS_SLAB:
                    rows = value.astype(f32)
                    bias[core] = bias[core] + (rows[:2] + rows[2:4])
                else:
                    row, lane = run * F_RUN + (slab // 2) * 16, core * HALF + (slab % 2) * 128
                    weight_ref[row : row + 16, lane : lane + 128] = value
    bias_ref[:2, :] = bias[0]
    bias_ref[2:, :] = bias[1]


def assemble(ids, mine, other):
    return pl.pallas_call(
        assemble_kernel,
        in_specs=[SMEM_SPEC] + [VMEM_SPEC] * 2,
        out_shape=(
            jax.ShapeDtypeStruct((RUN * F_RUN, HID), bf16),
            jax.ShapeDtypeStruct((4, 128), f32),
        ),
        name="assemble",
    )(ids, mine, other)


def high_low(value):
    high = lax.reduce_precision(value, 8, 7)
    return jnp.concatenate([high, value - high, jnp.zeros((12, 128), f32)], axis=0).astype(bf16)


def on_device(features, weight, bias, tile_cols, tile_count, nbr_slot, nbr_col, nbr_keep, upstream):
    group = (lax.axis_index("yh") * 4 + lax.axis_index("x")) * 8 + lax.axis_index("z")
    core = lax.axis_index("c")
    first = core == 0
    far_low, far_high = group % 32 == 0, group % 32 == 31
    ids = jnp.stack([group, lax.axis_index("yl"), core, far_low, far_high]).astype(i32)

    copies, same, cross = project(
        ids, tile_count, tile_cols, nbr_slot.T, nbr_col.T, nbr_keep.T, features, weight
    )
    straight, turned = across(same, cross)
    own = lax.all_to_all(copies, ("yl", "c"), 0, 0)
    tied, _ = lax.optimization_barrier((upstream, copies))
    up_other = swap_core(jnp.where(first, tied[:, HALF:], tied[:, :HALF]))
    slices = features.T.reshape(RUN, F_RUN, TILE)
    own, up_other, slices = lax.optimization_barrier((own, up_other, slices))
    straight, turned, _ = lax.optimization_barrier((straight, turned, own))
    received = jnp.stack([jnp.where(first, straight, turned), jnp.where(first, turned, straight)])
    low, high = neighbours(own)
    parts = along_run(received)
    counts, degree = forward_counts(ids, own)
    feats = lax.all_to_all(slices, "yl", 0, 0)
    feats_other = swap_core(feats)
    pieces = (own, low, high) + parts
    bias_half = jnp.where(first, bias[:HALF], bias[HALF:])[None]
    hidden_mine, hidden_send, scaled_copies, scaled, bias_part = forward_math(
        ids, counts, forward_own(ids, counts, own), degree, bias_half, upstream, up_other,
        pieces[1:],
    )

    received = across(scaled, None)
    own = lax.all_to_all(scaled_copies, "yl", 0, 0)
    hidden_got = swap_core(hidden_send)
    counts_back = backward_counts(ids, pieces)
    received, own, counts_back = lax.optimization_barrier((received, own, counts_back))
    own = own.reshape(MEMBERS, TILE, HALF)
    low, high = neighbours(own)
    parts = along_run(received)
    round_mine, round_send, slabs = backward_math(
        ids, counts_back, backward_own(counts_back, own), high_low(bias_part.reshape(2, 128)),
        feats, feats_other, (low, high) + parts,
    )
    round_got = swap_core(round_send)
    own_round = jnp.where(
        first,
        jnp.concatenate([round_mine, round_got], axis=1),
        jnp.concatenate([round_got, round_mine], axis=1),
    )
    grad_features = lax.dot_general(
        own_round, weight, (((1,), (1,)), ((), ())), preferred_element_type=f32
    ).astype(bf16)
    hidden = jnp.where(
        first,
        jnp.concatenate([hidden_mine, hidden_got], axis=1),
        jnp.concatenate([hidden_got, hidden_mine], axis=1),
    )
    terms = lax.all_to_all(slabs, WIDE, 0, 0)
    terms, grad_features, hidden = lax.optimization_barrier((terms, grad_features, hidden))
    reduced = jnp.sum(terms.astype(f32), axis=0)
    piece = jnp.where(
        group == BIAS_SLAB, high_low(reduced[:2] + reduced[2:4]), reduced.astype(bf16)
    )
    column = spread_to(piece, ("yh", "yl", "z"), 64)
    plane = spread_to(column, "x", 4)
    weight_grad, bias_grad = assemble(ids, plane, swap_core(plane))
    return hidden, grad_features, weight_grad, bias_grad.reshape(HID)


def solution(mesh):
    split = Mesh(mesh.devices.reshape(SIZES), AXES)
    rows = P(AXES, None)
    in_specs = (rows, P(), P(), rows, P(AXES), rows, rows, rows, rows)
    out_specs = (rows, rows, P(), P())
    return jax.shard_map(
        on_device, mesh=split, in_specs=in_specs, out_specs=out_specs, check_vma=False
    )
```
